128 devices in a mesh: replica: 16 (over x_lo, z, core), shard: 8 (over y, x_hi).
Axes of the slice: x: 4 (x_hi: 2, x_lo: 2; x = x_hi * 2 + x_lo), y: 4, z: 4, core: 2. Of those that a mesh axis runs over, the one named last changes fastest.
Arguments:
- weights: bfloat16 [16, 2560, 7168], P('replica', None, 'shard'), may hold values from -60 to 60, as said below
- inputs: bfloat16 [8192, 2560], P('replica'), may hold values from -0.125 to 0.125
- targets: bfloat16 [8192, 7168], P('replica', 'shard'), may hold values from -6 to 6
- factors: float32 [3, 7168, 16], P(None, 'shard'), may hold values from -6 to 6
Outputs:
- mixed: bfloat16 [16, 2560, 7168], P('replica', None, 'shard')
The draws below stay inside these ranges and needn't reach their ends.
Inputs may be any that keep to these rules, and one draw needn't show every extreme that they name: `weights`: independent entries for every replica.
All inputs are finite; a program needn't handle non-finite values.
Results may differ from the reference program's by a relative error of at most 0.0075.
Values may be sent and summed in bfloat16 or wider, within the bound.
A program may use at most 64 MiB of HBM per device.

```python
import jax
import jax.numpy as jnp
from jax import lax

D = 2560
FF = 7168
RANK = 16
ROUNDS = 3
TOK = 512
REPLICAS = 16
ROWS = 8192


def draw_weights(key, part):
    base = jax.random.truncated_normal(key, -6.0, 6.0, (REPLICAS, D, FF), jnp.float32)
    return base.astype(jnp.bfloat16)


def steps_of(stream_key, extent, split, low, largest):
    factor_of = 1.0
    for position, blocks in split:
        draws = jax.random.uniform(jax.random.fold_in(jax.random.fold_in(stream_key, 6), position), (blocks,), jnp.float32, low / len(split), largest / len(split))
        factor_of = factor_of * jnp.repeat(jnp.exp(draws), extent[position] // blocks).reshape((-1,) + (1,) * (len(extent) - 1 - position))
    return factor_of


def bell_draw(rng, dims, scale, reach, shards=(), held_as=jnp.bfloat16):
    array = scale * jax.random.normal(rng, dims, jnp.float32)
    if shards:
        array = array * steps_of(rng, dims, shards, -0.22, 0.18)
    return jnp.clip(array, -reach, reach).astype(held_as)


def setup_inputs(seed: int = 0) -> dict:
    key_of = jax.random.split(jax.random.key(seed), 5)
    weights = draw_weights(jax.random.fold_in(key_of[4], 71), 0)
    inputs = bell_draw(key_of[1], (ROWS, D), D ** -0.5, 0.125, ((0, 16),))
    targets = bell_draw(key_of[2], (ROWS, FF), 1.0, 6.0, ((0, 16), (1, 8)))
    factors = bell_draw(key_of[3], (ROUNDS, FF, RANK), 1.0, 6.0, ((1, 8),), jnp.float32)
    return dict(weights=weights, inputs=inputs, targets=targets, factors=factors)


DISTANCES = (1, 2, 4)
HIGH = lax.Precision.HIGHEST

def sgd_step(weight, rows_in, rows_target):
    output = jnp.dot(rows_in.astype(jnp.float32), weight.astype(jnp.float32), preferred_element_type=jnp.float32)
    resid = (output - rows_target.astype(jnp.float32)).astype(jnp.bfloat16)
    grad = jnp.dot(rows_in.T.astype(jnp.float32), resid.astype(jnp.float32), preferred_element_type=jnp.float32)
    return (weight.astype(jnp.float32) - 0.3 * grad).astype(jnp.bfloat16)

def orthonormal(diff):
    gram = jnp.dot(diff.T, diff, precision=HIGH)
    lower = jnp.linalg.cholesky(gram)
    solved = lax.linalg.triangular_solve(lower, diff, left_side=False, lower=True, transpose_a=True)
    return solved.astype(jnp.bfloat16)

def reference(weights, inputs, targets, factors):
    rows_in = inputs.reshape(REPLICAS, TOK, D)
    rows_target = targets.reshape(REPLICAS, TOK, FF)
    current = weights
    for step in range(ROUNDS):
        dist = DISTANCES[step]
        shared = factors[step].astype(jnp.bfloat16)

        def first_pass(index, carry):
            state, left = carry
            weight = lax.dynamic_index_in_dim(state, index, 0, keepdims=False)
            x_rows = lax.dynamic_index_in_dim(rows_in, index, 0, keepdims=False)
            t_rows = lax.dynamic_index_in_dim(rows_target, index, 0, keepdims=False)
            weight = sgd_step(weight, x_rows, t_rows)
            state = lax.dynamic_update_index_in_dim(state, weight, index, 0)
            product = jnp.dot(weight.astype(jnp.float32), shared.astype(jnp.float32), preferred_element_type=jnp.float32)
            left = lax.dynamic_update_index_in_dim(left, product, index, 0)
            return (state, left)
        left_init = jnp.zeros((REPLICAS, D, RANK), jnp.float32)
        current, left = lax.fori_loop(0, REPLICAS, first_pass, (current, left_init))
        diff = left - jnp.roll(left, dist, axis=0)
        basis = lax.map(orthonormal, diff)

        def second_pass(index, right):
            weight = lax.dynamic_index_in_dim(current, index, 0, keepdims=False)
            rows_basis = lax.dynamic_index_in_dim(basis, index, 0, keepdims=False)
            product = jnp.dot(weight.T.astype(jnp.float32), rows_basis.astype(jnp.float32), preferred_element_type=jnp.float32)
            return lax.dynamic_update_index_in_dim(right, product, index, 0)
        right = lax.fori_loop(0, REPLICAS, second_pass, jnp.zeros((REPLICAS, FF, RANK), jnp.float32))
        right_diff = right - jnp.roll(right, dist, axis=0)

        def third_pass(index, state):
            weight = lax.dynamic_index_in_dim(state, index, 0, keepdims=False)
            rows_basis = lax.dynamic_index_in_dim(basis, index, 0, keepdims=False)
            rows_right = lax.dynamic_index_in_dim(right_diff, index, 0, keepdims=False)
            delta = jnp.dot(rows_basis.astype(jnp.float32), rows_right.astype(jnp.bfloat16).T.astype(jnp.float32), preferred_element_type=jnp.float32)
            weight = (weight.astype(jnp.float32) - 0.5 * delta).astype(jnp.bfloat16)
            return lax.dynamic_update_index_in_dim(state, weight, index, 0)
        current = lax.fori_loop(0, REPLICAS, third_pass, current)
    return current
```

```python
import jax
import jax.numpy as jnp
from jax import lax
from jax.sharding import PartitionSpec as P

ROUNDS = 3
RANK = 16
DISTANCES = (1, 2, 4)
HIGH = lax.Precision.HIGHEST
F32, BF16 = jnp.float32, jnp.bfloat16
NT = (((1,), (1,)), ((), ()))
NN = (((1,), (0,)), ((), ()))
TN = (((0,), (0,)), ((), ()))


def mm(a, b, dims):
    return lax.dot_general(a.astype(BF16), b.astype(BF16), dims, preferred_element_type=F32)


def passed_along(value, axis, steps):
    count = lax.axis_size(axis)
    pairs = [(source, (source + steps) % count) for source in range(count)]
    return lax.ppermute(value, axis, pairs)


def orthonormal(diff):
    gram = lax.dot_general(diff, diff, NT, precision=HIGH, preferred_element_type=F32)
    lower = jnp.linalg.cholesky(gram)
    solved = lax.linalg.triangular_solve(lower, diff, left_side=True, lower=True)
    return solved.astype(BF16)


def per_device(weights, x, targets, factors):
    weight = weights[0]
    qb = factors.astype(BF16).transpose(0, 2, 1).reshape(ROUNDS * RANK, -1)
    partial = jnp.concatenate([mm(qb, weight, NT), mm(qb, targets, NT)], axis=1)
    total = lax.psum(partial, "shard")
    depth = weight.shape[0]
    shared, goal = total[:, :depth], total[:, depth:]

    first = mm(x, weight, NN) - targets.astype(F32)
    gram_x = mm(x, x, NT)
    sums = [first]
    for _ in range(ROUNDS - 1):
        sums.append(first + sums[-1] - 0.3 * mm(gram_x, sums[-1], NN))
    grown = weight.astype(F32) - 0.3 * mm(x, sums[-1], TN)

    bases, rights = [], []
    for step in range(ROUNDS):
        dist = DISTANCES[step]
        shared = shared - 0.3 * mm(mm(shared, x, NT) - goal, x, NN)
        left = shared[:RANK]
        basis = orthonormal(left - passed_along(left, "replica", dist))
        shared, goal = shared[RANK:], goal[RANK:]
        if step < ROUNDS - 1:
            inner = mm(shared, basis, NT)
            inner = inner - passed_along(inner, "replica", dist)
            shared = shared - 0.5 * mm(inner, basis, NN)
        inside = mm(basis, x, NT)
        right = mm(basis, weight, NN) - 0.3 * mm(inside, sums[step], NN)
        for old, old_right in zip(bases, rights):
            right = right - 0.5 * mm(mm(basis, old, NT), old_right, NN)
        rights.append(right - passed_along(right, "replica", dist))
        bases.append(basis)
        if step < ROUNDS - 1:
            bases = [old.astype(F32) - 0.3 * mm(mm(old, x, NT), x, NN) for old in bases]
    low_rank = mm(jnp.concatenate([b.astype(F32) for b in bases]), jnp.concatenate(rights), TN)
    return (grown - 0.5 * low_rank).astype(BF16)[None]


def solution(mesh):
    in_specs = (
        P("replica", None, "shard"),
        P("replica", None),
        P("replica", "shard"),
        P(None, "shard", None),
    )
    out_specs = P("replica", None, "shard")
    return jax.shard_map(
        per_device, mesh=mesh, in_specs=in_specs, out_specs=out_specs, check_vma=False
    )
```

```python
import jax
import jax.numpy as jnp
from jax import lax
from jax.experimental import pallas as pl
from jax.experimental.pallas import tpu as pltpu
from jax.sharding import PartitionSpec as P

RANK = 16
DISTANCES = (1, 2, 4)
HIGH = lax.Precision.HIGHEST
F32, BF16 = jnp.float32, jnp.bfloat16
NT = (((1,), (1,)), ((), ()))
NN = (((1,), (0,)), ((), ()))
TN = (((0,), (0,)), ((), ()))
MESH = pl.DeviceIdType.MESH
CHUNK = 512


def mm(a, b, dims):
    return lax.dot_general(a.astype(BF16), b.astype(BF16), dims, preferred_element_type=F32)


def stacked(value):
    high = value.astype(BF16)
    rest = (value - high.astype(F32)).astype(BF16)
    return jnp.concatenate([high, rest], axis=0)


def folded(product):
    half = product.shape[0] // 2
    return product[:half] + product[half:]


def fine(value, matrix, dims):
    return folded(lax.dot_general(stacked(value), matrix, dims, preferred_element_type=F32))


def inverse_factor(gram):
    lane = lax.broadcasted_iota(jnp.int32, (RANK, RANK), 1)
    row = lax.broadcasted_iota(jnp.int32, (RANK, RANK), 0)
    below = lax.broadcasted_iota(jnp.int32, (RANK, 1), 0)
    inverse = jnp.where(lane == row, 1.0, 0.0).astype(F32)
    pivots = jnp.ones((RANK, 1), F32)
    for j in range(RANK):
        pivot = gram[j : j + 1, j : j + 1]
        factor = jnp.where(below > j, gram[:, j : j + 1] / pivot, 0.0)
        pivots = jnp.where(below == j, pivot, pivots)
        inverse = inverse - factor * inverse[j : j + 1, :]
        gram = gram - factor * gram[j : j + 1, :]
    return lax.rsqrt(pivots) * inverse


def orthonormal(diff):
    gram = lax.dot_general(diff, diff, NT, precision=HIGH, preferred_element_type=F32)
    inverse = inverse_factor(gram)
    basis = lax.dot_general(inverse, diff, NN, precision=HIGH, preferred_element_type=F32)
    return basis.astype(BF16)


def make_kernel(replicas, shards, depth, hidden, tokens):
    wide = depth + tokens
    lanes = wide // shards
    part_lanes = depth // (shards // 2)

    def kernel(
        w_hbm, x_hbm, t_hbm, f_ref, grown_hbm, bases_ref, rights_ref,
        w, x, t, first, sums, gram_x, grown,
        part0, part1, rs0, rs1, own0, own1, p_own, p_in, v12, c_out, c_in, q_out, q_in,
        load_sem, rs_send, rs_recv, ag_send, ag_recv, x_send, x_recv,
    ):
        r, s = lax.axis_index("replica"), lax.axis_index("shard")

        def peer(dr, ds):
            return (lax.rem(r + (dr + replicas), replicas), lax.rem(s + ds, shards))

        def load(source, target, number):
            return pltpu.make_async_copy(source, target, load_sem.at[number])

        def send(source, target, send_sem, recv_sem, where):
            return pltpu.make_async_remote_copy(
                src_ref=source, dst_ref=target, send_sem=send_sem, recv_sem=recv_sem,
                device_id=where, device_id_type=MESH,
            )

        chunks = depth // CHUNK
        loads = [
            load(w_hbm.at[pl.ds(c * CHUNK, CHUNK)], w.at[pl.ds(c * CHUNK, CHUNK)], c)
            for c in range(chunks)
        ] + [load(t_hbm, t, chunks), load(x_hbm, x, chunks + 1)]
        for copy in loads:
            copy.start()

        barrier = pltpu.get_barrier_semaphore()
        friends = [(0, o) for o in range(1, shards)]
        friends += [(1, o) for o in range(shards)] + [(-1, o) for o in range(shards)]
        friends += [(2, 0), (-2, 0), (4, 0), (-4, 0)]
        for dr, ds in friends:
            pl.semaphore_signal(barrier, inc=1, device_id=peer(dr, ds), device_id_type=MESH)

        c_out[...] = jnp.zeros_like(c_out)
        shared = f_ref[...].astype(BF16)
        images = []
        for c in range(chunks):
            loads[c].wait()
            images.append(lax.dot_general(shared, w[c * CHUNK : (c + 1) * CHUNK, :], NT, preferred_element_type=F32))
        loads[chunks].wait()
        goal = lax.dot_general(shared, t[...], NT, preferred_element_type=F32)
        loads[chunks + 1].wait()
        image = jnp.concatenate(images, axis=1)

        def stepped(value, aim):
            off = fine(value, x[...], NT) - aim
            return value - 0.3 * fine(off, x[...], NN)

        image = stepped(image, goal)
        part0[...] = image[:RANK]
        part1[:, :depth] = image[RANK:]
        part1[:, depth:] = goal[RANK:]

        def piece0(ref, index):
            rows = pl.multiple_of(lax.rem(index, 2) * 8, 8)
            columns = pl.multiple_of((index // 2) * part_lanes, 128)
            return ref.at[pl.ds(rows, 8), pl.ds(columns, part_lanes)]

        def piece1(ref, index):
            columns = pl.multiple_of(index * lanes, 128)
            return ref.at[:, pl.ds(columns, lanes)]

        pl.semaphore_wait(barrier, len(friends))
        scatter0, scatter1 = [], []
        for o in range(1, shards):
            where = peer(0, o)
            scatter0.append(send(piece0(part0, where[1]), rs0.at[o], rs_send.at[0, o], rs_recv.at[0, o], where))
            scatter0[-1].start()
        for o in range(1, shards):
            where = peer(0, o)
            scatter1.append(send(piece1(part1, where[1]), rs1.at[o], rs_send.at[1, o], rs_recv.at[1, o], where))
            scatter1[-1].start()

        def first_columns(j, carry):
            columns = pl.ds(pl.multiple_of(j * 128, 128), 128)
            product = lax.dot_general(x[...], w[:, columns], NN, preferred_element_type=F32)
            product = product - t[:, columns].astype(F32)
            first[:, columns] = product
            sums[0, :, columns] = product.astype(BF16)
            return carry

        lax.fori_loop(0, hidden // 128, first_columns, 0)

        for copy in scatter0:
            copy.wait_recv()
        total = piece0(part0, s)[...]
        for o in range(1, shards):
            total = total + rs0[o]
        own0[...] = total
        piece0(p_own, s)[...] = total
        gather0 = []
        for dr, o in [(0, o) for o in range(1, shards)] + [(1, o) for o in range(shards)]:
            target = piece0(p_own if dr == 0 else p_in.at[0], s)
            number = o if dr == 0 else shards + o
            gather0.append(send(own0, target, ag_send.at[number], ag_recv.at[number], peer(dr, o)))
            gather0[-1].start()
        for copy in scatter1:
            copy.wait_recv()
        total = piece1(part1, s)[...]
        for o in range(1, shards):
            total = total + rs1[o]
        own1[...] = total
        piece1(v12, s)[...] = total
        gather1 = []
        for o in range(1, shards):
            number = 2 * shards + o
            gather1.append(send(own1, piece1(v12, s), ag_send.at[number], ag_recv.at[number], peer(0, o)))
            gather1[-1].start()

        def gram_columns(j, carry):
            columns = pl.ds(pl.multiple_of(j * 128, 128), 128)
            gram_x[:, columns] = lax.dot_general(
                x[...], x[columns, :], NT, preferred_element_type=F32
            ).astype(BF16)
            return carry

        lax.fori_loop(0, tokens // 128, gram_columns, 0)

        def next_sum(step):
            def columns_of(j, carry):
                columns = pl.ds(pl.multiple_of(j * 128, 128), 128)
                last = sums[step - 1, :, columns]
                product = lax.dot_general(gram_x[...], last, NN, preferred_element_type=F32)
                sums[step, :, columns] = (first[:, columns] + last.astype(F32) - 0.3 * product).astype(BF16)
                return carry

            lax.fori_loop(0, hidden // 128, columns_of, 0)

        def exchange(source, target, kind, step):
            copy = send(source, target, x_send.at[kind, step], x_recv.at[kind, step], peer(DISTANCES[step], 0))
            copy.start()
            return copy

        for copy in gather0:
            copy.wait_recv()
        basis0 = orthonormal(p_own[...] - p_in[0])
        for copy in gather1:
            copy.wait_recv()
        image, goal = v12[:, :depth], v12[:, depth:]
        inner0 = fine(image, basis0, NT)
        c_out[0, :, :RANK] = inner0
        sent_c0 = exchange(c_out.at[0], c_in.at[0], 0, 0)

        inside0 = lax.dot_general(basis0, x[...], NT, preferred_element_type=F32)
        image = stepped(image, goal)
        moved0 = basis0.astype(F32) - 0.3 * fine(inside0, x[...], NN)
        sent_c0.wait_recv()
        inner0 = inner0 - c_in[0, :, :RANK]
        image = image - 0.5 * lax.dot_general(inner0, moved0, NN, precision=HIGH, preferred_element_type=F32)
        p_in_1 = image[:RANK]
        for copy in scatter0:
            copy.wait_send()
        part0[...] = p_in_1
        sent_p1 = exchange(part0, p_in.at[1], 1, 1)

        right0 = lax.dot_general(basis0, w[...], NN, preferred_element_type=F32)
        right0 = right0 - 0.3 * mm(inside0, sums[0], NN)
        q_out[0] = right0
        sent_q0 = exchange(q_out.at[0], q_in.at[0], 2, 0)
        next_sum(1)

        image, goal = image[RANK:], goal[RANK:]
        sent_p1.wait_recv()
        basis1 = orthonormal(p_in_1 - p_in[1])
        inner1 = fine(image, basis1, NT)
        c_out[1, :RANK, :RANK] = inner1
        sent_c1 = exchange(c_out.at[1], c_in.at[1], 0, 1)
        inside1 = lax.dot_general(basis1, x[...], NT, preferred_element_type=F32)
        image = stepped(image, goal)
        moved1 = basis1.astype(F32) - 0.3 * fine(inside1, x[...], NN)
        sent_c1.wait_recv()
        inner1 = inner1 - c_in[1, :RANK, :RANK]
        image = image - 0.5 * lax.dot_general(inner1, moved1, NN, precision=HIGH, preferred_element_type=F32)
        for copy in gather0:
            copy.wait_send()
        p_own[...] = image
        sent_p2 = exchange(p_own, p_in.at[2], 1, 2)

        sent_q0.wait_recv()
        right0 = right0 - q_in[0]
        right1 = lax.dot_general(basis1, w[...], NN, preferred_element_type=F32)
        right1 = right1 - 0.3 * mm(inside1, sums[1], NN) - 0.5 * mm(mm(basis1, moved0, NT), right0, NN)
        q_out[1] = right1
        sent_q1 = exchange(q_out.at[1], q_in.at[1], 2, 1)
        twice0 = moved0 - 0.3 * fine(fine(moved0, x[...], NT), x[...], NN)
        next_sum(2)

        def grown_rows(j, carry):
            rows = pl.ds(pl.multiple_of(j * 256, 256), 256)
            product = lax.dot_general(x[:, rows], sums[2], TN, preferred_element_type=F32)
            grown[rows, :] = (w[rows, :].astype(F32) - 0.3 * product).astype(BF16)
            return carry

        lax.fori_loop(0, depth // 256, grown_rows, 0)
        written = pltpu.make_async_copy(grown, grown_hbm, load_sem.at[chunks + 2])
        written.start()

        sent_p2.wait_recv()
        basis2 = orthonormal(image - p_in[2])
        sent_q1.wait_recv()
        right1 = right1 - q_in[1]
        right2 = lax.dot_general(basis2, grown[...], NN, preferred_element_type=F32)
        right2 = right2 - 0.5 * mm(mm(basis2, twice0, NT), right0, NN)
        right2 = right2 - 0.5 * mm(mm(basis2, moved1, NT), right1, NN)
        q_out[2] = right2
        sent_q2 = exchange(q_out.at[2], q_in.at[2], 2, 2)
        bases_ref[:RANK, :] = twice0.astype(BF16)
        bases_ref[RANK : 2 * RANK, :] = moved1.astype(BF16)
        bases_ref[2 * RANK :, :] = basis2
        rights_ref[:RANK, :] = right0.astype(BF16)
        rights_ref[RANK : 2 * RANK, :] = right1.astype(BF16)
        for copy in scatter1 + gather1 + [sent_c0, sent_c1, sent_p1, sent_p2, sent_q0, sent_q1]:
            copy.wait_send()
        written.wait()
        sent_q2.wait_recv()
        rights_ref[2 * RANK :, :] = (right2 - q_in[2]).astype(BF16)
        sent_q2.wait_send()

    vm, dma = pltpu.VMEM, pltpu.SemaphoreType.DMA
    scratch = [
        vm((depth, hidden), BF16), vm((tokens, depth), BF16), vm((tokens, hidden), BF16),
        vm((tokens, hidden), F32), vm((3, tokens, hidden), BF16), vm((tokens, tokens), BF16),
        vm((depth, hidden), BF16),
        vm((RANK, depth), F32), vm((2 * RANK, wide), F32),
        vm((shards, 8, part_lanes), F32), vm((shards, 2 * RANK, lanes), F32),
        vm((8, part_lanes), F32), vm((2 * RANK, lanes), F32),
        vm((RANK, depth), F32), vm((3, RANK, depth), F32), vm((2 * RANK, wide), F32),
        vm((2, 2 * RANK, 128), F32), vm((2, 2 * RANK, 128), F32),
        vm((3, RANK, hidden), F32), vm((3, RANK, hidden), F32),
        dma((depth // CHUNK + 3,)), dma((2, shards)), dma((2, shards)),
        dma((3 * shards,)), dma((3 * shards,)), dma((3, 3)), dma((3, 3)),
    ]
    return kernel, scratch


def solution(mesh):
    replicas, shards = mesh.shape["replica"], mesh.shape["shard"]

    def per_device(weights, x, targets, factors):
        weight = weights[0]
        depth, hidden = weight.shape
        tokens = x.shape[0]
        shared = factors.transpose(0, 2, 1).reshape(3 * RANK, hidden)
        kernel, scratch = make_kernel(replicas, shards, depth, hidden, tokens)
        in_vmem = pl.BlockSpec(memory_space=pltpu.VMEM)
        anywhere = pl.BlockSpec(memory_space=pl.ANY)
        grown, bases, rights = pl.pallas_call(
            kernel,
            out_shape=(
                jax.ShapeDtypeStruct((depth, hidden), BF16),
                jax.ShapeDtypeStruct((3 * RANK, depth), BF16),
                jax.ShapeDtypeStruct((3 * RANK, hidden), BF16),
            ),
            in_specs=[anywhere, anywhere, anywhere, in_vmem],
            out_specs=(anywhere, in_vmem, in_vmem),
            scratch_shapes=scratch,
            compiler_params=pltpu.CompilerParams(
                collective_id=0, has_side_effects=True, vmem_limit_bytes=56 * 2**20
            ),
            name="rounds",
        )(weight, x, targets, shared)
        delta = lax.dot_general(bases, rights, TN, preferred_element_type=F32)
        return (grown.astype(F32) - 0.5 * delta).astype(BF16)[None]

    in_specs = (
        P("replica", None, "shard"),
        P("replica", None),
        P("replica", "shard"),
        P(None, "shard", None),
    )
    return jax.shard_map(
        per_device, mesh=mesh, in_specs=in_specs, out_specs=P("replica", None, "shard"), check_vma=False
    )
```

```python
import jax
import jax.numpy as jnp
from jax import lax
from jax.experimental import pallas as pl
from jax.experimental.pallas import tpu as pltpu
from jax.sharding import PartitionSpec as P

RANK = 16
DISTANCES = (1, 2, 4)
F32, BF16 = jnp.float32, jnp.bfloat16
NT = (((1,), (1,)), ((), ()))
NN = (((1,), (0,)), ((), ()))
TN = (((0,), (0,)), ((), ()))
MESH = pl.DeviceIdType.MESH
CHUNK = 512


def mm(a, b, dims):
    return lax.dot_general(a.astype(BF16), b.astype(BF16), dims, preferred_element_type=F32)


def inverse_factor(gram):
    shape = (RANK, 128)
    lane = lax.broadcasted_iota(jnp.int32, shape, 1)
    row = lax.broadcasted_iota(jnp.int32, shape, 0)
    inverse = jnp.where(lane == row, 1.0, 0.0).astype(F32)
    columns = [jnp.broadcast_to(gram[:, k : k + 1], shape) for k in range(RANK)]
    pivots = jnp.ones(shape, F32)
    for j in range(RANK):
        pivot = jnp.broadcast_to(columns[j][j : j + 1, :], shape)
        pivots = jnp.where(row == j, pivot, pivots)
        if j < RANK - 1:
            factor = jnp.where(row > j, columns[j] / pivot, 0.0)
            for k in range(j + 1, RANK):
                columns[k] = columns[k] - factor * jnp.broadcast_to(columns[k][j : j + 1, :], shape)
            inverse = inverse - factor * jnp.broadcast_to(inverse[j : j + 1, :], shape)
    return (lax.rsqrt(pivots) * inverse)[:, :RANK]


def orthonormal(diff):
    high = diff.astype(BF16)
    rest = diff - high.astype(F32)
    middle = rest.astype(BF16)
    low = (rest - middle.astype(F32)).astype(BF16)
    pieces = jnp.concatenate([high, middle, low], axis=0)
    gram = lax.dot_general(pieces, pieces, NT, preferred_element_type=F32)
    gram = gram[:RANK] + gram[RANK : 2 * RANK] + gram[2 * RANK :]
    gram = gram[:, :RANK] + gram[:, RANK : 2 * RANK] + gram[:, 2 * RANK :]
    inverse = inverse_factor(gram)
    top = inverse.astype(BF16)
    inverse = jnp.concatenate([top, (inverse - top.astype(F32)).astype(BF16)], axis=0)
    basis = lax.dot_general(inverse, high, NN, preferred_element_type=F32)
    basis = basis + lax.dot_general(inverse, middle, NN, preferred_element_type=F32)
    return (basis[:RANK] + basis[RANK:]).astype(BF16)


def make_kernel(replicas, shards, depth, hidden, tokens):
    wide = depth + tokens
    lanes = wide // shards
    blocks = [(c, min(256, hidden - c)) for c in range(0, hidden, 256)]

    def kernel(
        w_hbm, x_hbm, t_hbm, f_hbm, grown, bases_ref, rights_ref,
        f, w, x, t, first, sums, gram_x,
        part0, part1, rs0, rs1, own0, own1, p_own, p0_in, p_out, p_in, v12, c_out, c_in, q_out, q_in,
        load_sem, rs_send, rs_recv, ag_send, ag_recv, x_send, x_recv,
    ):
        r, s = lax.axis_index("replica"), lax.axis_index("shard")

        def peer(dr, ds):
            return (lax.rem(r + (dr + replicas), replicas), lax.rem(s + ds, shards))

        def load(source, target, number):
            return pltpu.make_async_copy(source, target, load_sem.at[number])

        def send(source, target, send_sem, recv_sem, where):
            return pltpu.make_async_remote_copy(
                src_ref=source, dst_ref=target, send_sem=send_sem, recv_sem=recv_sem,
                device_id=where, device_id_type=MESH,
            )

        chunks = depth // CHUNK
        loads = [load(f_hbm, f, chunks + 2)]
        loads += [
            load(w_hbm.at[pl.ds(c * CHUNK, CHUNK)], w.at[pl.ds(c * CHUNK, CHUNK)], c)
            for c in range(chunks)
        ]
        loads += [load(t_hbm, t, chunks), load(x_hbm, x, chunks + 1)]
        for copy in loads:
            copy.start()

        barrier = pltpu.get_barrier_semaphore()
        friends = [(0, o) for o in range(1, shards)]
        friends += [(1, o) for o in range(shards)] + [(-1, o) for o in range(shards)]
        friends += [(2, 0), (-2, 0), (4, 0), (-4, 0)]
        for dr, ds in friends:
            pl.semaphore_signal(barrier, inc=1, device_id=peer(dr, ds), device_id_type=MESH)

        c_out[...] = jnp.zeros_like(c_out)
        loads[0].wait()
        shared = f[...].astype(BF16)
        images = []
        for c in range(chunks):
            loads[1 + c].wait()
            images.append(mm(shared, w[c * CHUNK : (c + 1) * CHUNK, :], NT))
        loads[1 + chunks].wait()
        goal = mm(shared, t[...], NT)
        loads[2 + chunks].wait()
        image = jnp.concatenate(images, axis=1)
        image = image - 0.3 * mm(mm(image, x[...], NT) - goal, x[...], NN)
        image, goal = image.astype(BF16), goal.astype(BF16)
        part0[:, :depth] = image[:RANK]
        part0[:, depth:] = goal[:RANK]
        part1[:, :depth] = image[RANK:]
        part1[:, depth:] = goal[RANK:]

        def piece(ref, index):
            return ref.at[:, pl.ds(pl.multiple_of(index * lanes, 128), lanes)]

        pl.semaphore_wait(barrier, len(friends))
        scatter0, scatter1 = [], []
        for o in range(1, shards):
            where = peer(0, o)
            scatter0.append(send(piece(part0, where[1]), rs0.at[o], rs_send.at[0, o], rs_recv.at[0, o], where))
            scatter0[-1].start()
        for o in range(1, shards):
            where = peer(0, o)
            scatter1.append(send(piece(part1, where[1]), rs1.at[o], rs_send.at[1, o], rs_recv.at[1, o], where))
            scatter1[-1].start()

        for c, width in blocks:
            product = mm(x[...], w[:, c : c + width], NN) - t[:, c : c + width].astype(F32)
            first[:, c : c + width] = product
            sums[0, :, c : c + width] = product.astype(BF16)

        for copy in scatter0:
            copy.wait_recv()
        total = piece(part0, s)[...].astype(F32)
        for o in range(1, shards):
            total = total + rs0[o].astype(F32)
        own0[...] = total.astype(BF16)
        piece(p_own, s)[...] = total.astype(BF16)
        gather0 = []
        for dr, o in [(0, o) for o in range(1, shards)] + [(1, o) for o in range(shards)]:
            target = piece(p_own if dr == 0 else p0_in, s)
            number = o if dr == 0 else shards + o
            gather0.append(send(own0, target, ag_send.at[number], ag_recv.at[number], peer(dr, o)))
            gather0[-1].start()
        for copy in scatter1:
            copy.wait_recv()
        total = piece(part1, s)[...].astype(F32)
        for o in range(1, shards):
            total = total + rs1[o].astype(F32)
        own1[...] = total.astype(BF16)
        piece(v12, s)[...] = total.astype(BF16)
        gather1 = []
        for o in range(1, shards):
            number = 2 * shards + o
            gather1.append(send(own1, piece(v12, s), ag_send.at[number], ag_recv.at[number], peer(0, o)))
            gather1[-1].start()

        for c in range(0, tokens, 256):
            gram_x[:, c : c + 256] = mm(x[...], x[c : c + 256, :], NT).astype(BF16)
        for step in (1, 2):
            for c, width in blocks:
                last = sums[step - 1, :, c : c + width]
                product = mm(gram_x[...], last, NN)
                value = first[:, c : c + width] + last.astype(F32) - 0.3 * product
                sums[step, :, c : c + width] = value.astype(BF16)

        def grow(c):
            rows = slice(c * CHUNK, (c + 1) * CHUNK)
            product = mm(x[:, rows], sums[2], TN)
            grown[rows, :] = (w[rows, :].astype(F32) - 0.3 * product).astype(BF16)

        def exchange(source, target, kind, step):
            copy = send(source, target, x_send.at[kind, step], x_recv.at[kind, step], peer(DISTANCES[step], 0))
            copy.start()
            return copy

        for copy in gather0:
            copy.wait_recv()
        basis0 = orthonormal(p_own[:, :depth].astype(F32) - p0_in[:, :depth].astype(F32))
        for copy in gather1:
            copy.wait_recv()
        image = v12[:, :depth]
        inner0 = mm(image, basis0, NT)
        c_out[0, :, :RANK] = inner0
        sent_c0 = exchange(c_out.at[0], c_in.at[0], 0, 0)
        inside = mm(jnp.concatenate([image, basis0], axis=0), x[...], NT)
        inside0 = inside[2 * RANK :]
        inside = jnp.concatenate([inside[: 2 * RANK] - v12[:, depth:].astype(F32), inside0], axis=0)
        change = 0.3 * mm(inside, x[...], NN)
        image = image.astype(F32) - change[: 2 * RANK]
        moved0 = basis0.astype(F32) - change[2 * RANK :]
        sent_c0.wait_recv()
        inner0 = inner0 - c_in[0, :, :RANK]
        image = image - 0.5 * mm(inner0, moved0, NN)
        left1 = image[:RANK]
        p_out[0] = left1.astype(BF16)
        sent_p1 = exchange(p_out.at[0], p_in.at[0], 1, 1)

        right0 = mm(basis0, w[...], NN) - 0.3 * mm(inside0, sums[0], NN)
        q_out[0] = right0.astype(BF16)
        sent_q0 = exchange(q_out.at[0], q_in.at[0], 2, 0)
        image = image[RANK:]
        inside = mm(jnp.concatenate([image, moved0], axis=0), x[...], NT)
        inside = jnp.concatenate([inside[:RANK] - v12[RANK:, depth:].astype(F32), inside[RANK:]], axis=0)
        change = 0.3 * mm(inside, x[...], NN)
        next_image = image - change[:RANK]
        twice0 = moved0 - change[RANK:]
        grow(0)
        grow(1)

        sent_p1.wait_recv()
        basis1 = orthonormal(left1 - p_in[0].astype(F32))
        inner1 = mm(image, basis1, NT)
        c_out[1, :RANK, :RANK] = inner1
        sent_c1 = exchange(c_out.at[1], c_in.at[1], 0, 1)
        inside1 = mm(basis1, x[...], NT)
        moved1 = basis1.astype(F32) - 0.3 * mm(inside1, x[...], NN)
        sent_c1.wait_recv()
        inner1 = inner1 - c_in[1, :RANK, :RANK]
        left2 = next_image - 0.5 * mm(inner1, moved1, NN)
        p_out[1] = left2.astype(BF16)
        sent_p2 = exchange(p_out.at[1], p_in.at[1], 1, 2)

        sent_q0.wait_recv()
        right0 = right0 - q_in[0].astype(F32)
        right1 = mm(basis1, w[...], NN) - 0.3 * mm(inside1, sums[1], NN)
        right1 = right1 - 0.5 * mm(mm(basis1, moved0, NT), right0, NN)
        q_out[1] = right1.astype(BF16)
        sent_q1 = exchange(q_out.at[1], q_in.at[1], 2, 1)
        for c in range(2, chunks):
            grow(c)
        bases_ref[:RANK, :] = twice0.astype(BF16)
        bases_ref[RANK : 2 * RANK, :] = moved1.astype(BF16)
        rights_ref[:RANK, :] = right0.astype(BF16)

        sent_p2.wait_recv()
        basis2 = orthonormal(left2 - p_in[1].astype(F32))
        sent_q1.wait_recv()
        right1 = right1 - q_in[1].astype(F32)
        right2 = mm(basis2, grown[...], NN)
        right2 = right2 - 0.5 * mm(mm(basis2, twice0, NT), right0, NN)
        right2 = right2 - 0.5 * mm(mm(basis2, moved1, NT), right1, NN)
        q_out[2] = right2.astype(BF16)
        sent_q2 = exchange(q_out.at[2], q_in.at[2], 2, 2)
        bases_ref[2 * RANK :, :] = basis2
        rights_ref[RANK : 2 * RANK, :] = right1.astype(BF16)
        started = scatter0 + scatter1 + gather0 + gather1
        for copy in started + [sent_c0, sent_c1, sent_p1, sent_p2, sent_q0, sent_q1]:
            copy.wait_send()
        sent_q2.wait_recv()
        rights_ref[2 * RANK :, :] = (right2 - q_in[2].astype(F32)).astype(BF16)
        sent_q2.wait_send()

    vm, dma = pltpu.VMEM, pltpu.SemaphoreType.DMA
    scratch = [
        vm((3 * RANK, hidden), F32), vm((depth, hidden), BF16), vm((tokens, depth), BF16), vm((tokens, hidden), BF16),
        vm((tokens, hidden), F32), vm((3, tokens, hidden), BF16), vm((tokens, tokens), BF16),
        vm((RANK, wide), BF16), vm((2 * RANK, wide), BF16),
        vm((shards, RANK, lanes), BF16), vm((shards, 2 * RANK, lanes), BF16),
        vm((RANK, lanes), BF16), vm((2 * RANK, lanes), BF16),
        vm((RANK, wide), BF16), vm((RANK, wide), BF16), vm((2, RANK, depth), BF16), vm((2, RANK, depth), BF16),
        vm((2 * RANK, wide), BF16),
        vm((2, 2 * RANK, 128), F32), vm((2, 2 * RANK, 128), F32),
        vm((3, RANK, hidden), BF16), vm((3, RANK, hidden), BF16),
        dma((depth // CHUNK + 3,)), dma((2, shards)), dma((2, shards)),
        dma((3 * shards,)), dma((3 * shards,)), dma((3, 3)), dma((3, 3)),
    ]
    return kernel, scratch


def solution(mesh):
    replicas, shards = mesh.shape["replica"], mesh.shape["shard"]

    def per_device(weights, x, targets, factors):
        weight = weights[0]
        depth, hidden = weight.shape
        tokens = x.shape[0]
        shared = factors.transpose(0, 2, 1).reshape(3 * RANK, hidden)
        kernel, scratch = make_kernel(replicas, shards, depth, hidden, tokens)
        in_vmem = pl.BlockSpec(memory_space=pltpu.VMEM)
        grown, bases, rights = pl.pallas_call(
            kernel,
            out_shape=(
                pltpu.VMEM((depth, hidden), BF16),
                jax.ShapeDtypeStruct((3 * RANK, depth), BF16),
                jax.ShapeDtypeStruct((3 * RANK, hidden), BF16),
            ),
            in_specs=[pl.BlockSpec(memory_space=pltpu.HBM)] * 4,
            out_specs=(in_vmem, in_vmem, in_vmem),
            scratch_shapes=scratch,
            compiler_params=pltpu.CompilerParams(
                collective_id=0, has_side_effects=True, vmem_limit_bytes=40 * 2**20
            ),
            name="rounds",
        )(*(pltpu.with_memory_space_constraint(v, pltpu.HBM) for v in (weight, x, targets, shared)))
        delta = lax.dot_general(bases, rights, TN, preferred_element_type=F32)
        return (grown.astype(F32) - 0.5 * delta).astype(BF16)[None]

    in_specs = (
        P("replica", None, "shard"),
        P("replica", None),
        P("replica", "shard"),
        P(None, "shard", None),
    )
    return jax.shard_map(
        per_device, mesh=mesh, in_specs=in_specs, out_specs=P("replica", None, "shard"), check_vma=False
    )
```

```python
import jax
import jax.numpy as jnp
from jax import lax
from jax.experimental import pallas as pl
from jax.experimental.pallas import tpu as pltpu
from jax.sharding import PartitionSpec as P

RANK = 16
F32, BF16 = jnp.float32, jnp.bfloat16
NT = (((1,), (1,)), ((), ()))
NN = (((1,), (0,)), ((), ()))
TN = (((0,), (0,)), ((), ()))
MESH = pl.DeviceIdType.MESH
CHUNK = 512


def mm(a, b, dims):
    return lax.dot_general(a.astype(BF16), b.astype(BF16), dims, preferred_element_type=F32)


def inverse_factor(gram):
    shape = (RANK, 128)
    lane = lax.broadcasted_iota(jnp.int32, shape, 1)
    row = lax.broadcasted_iota(jnp.int32, shape, 0)
    inverse = jnp.where(lane == row, 1.0, 0.0).astype(F32)
    columns = [jnp.broadcast_to(gram[:, k : k + 1], shape) for k in range(RANK)]
    pivots = jnp.ones(shape, F32)
    for j in range(RANK):
        pivot = jnp.broadcast_to(columns[j][j : j + 1, :], shape)
        pivots = jnp.where(row == j, pivot, pivots)
        if j < RANK - 1:
            factor = jnp.where(row > j, columns[j] / pivot, 0.0)
            for k in range(j + 1, RANK):
                columns[k] = columns[k] - factor * jnp.broadcast_to(columns[k][j : j + 1, :], shape)
            inverse = inverse - factor * jnp.broadcast_to(inverse[j : j + 1, :], shape)
    return (lax.rsqrt(pivots) * inverse)[:, :RANK]


def product_of(inverse, value):
    high = value.astype(BF16)
    rest = (value - high.astype(F32)).astype(BF16)
    result = mm(inverse, high, NN) + mm(inverse, rest, NN)
    return result[:RANK] + result[RANK:]


def factored(diff):
    high = diff.astype(BF16)
    rest = diff - high.astype(F32)
    middle = rest.astype(BF16)
    low = (rest - middle.astype(F32)).astype(BF16)
    pieces = jnp.concatenate([high, middle, low], axis=0)
    gram = lax.dot_general(pieces, pieces, NT, preferred_element_type=F32)
    gram = gram[:RANK] + gram[RANK : 2 * RANK] + gram[2 * RANK :]
    gram = gram[:, :RANK] + gram[:, RANK : 2 * RANK] + gram[:, 2 * RANK :]
    inverse = inverse_factor(gram)
    top = inverse.astype(BF16)
    inverse = jnp.concatenate([top, (inverse - top.astype(F32)).astype(BF16)], axis=0)
    return inverse, pieces[: 2 * RANK]


def orthonormal(diff):
    inverse, _ = factored(diff)
    return product_of(inverse, diff).astype(BF16)


def update_kernel(grown, bases, rights, out_hbm, staged, sem):
    copies = []
    for number, c in enumerate(range(0, grown.shape[1], 256)):
        columns = pl.ds(c, min(256, grown.shape[1] - c))
        delta = mm(bases[...], rights[:, columns], TN)
        staged[:, columns] = (grown[:, columns].astype(F32) - 0.5 * delta).astype(BF16)
        copies.append(pltpu.make_async_copy(staged.at[:, columns], out_hbm.at[:, columns], sem.at[number]))
        copies[-1].start()
    for copy in copies:
        copy.wait()


def make_kernel(replicas, shards, depth, hidden, tokens):
    wide = depth + tokens
    lanes = wide // shards
    blocks = [(c, min(256, hidden - c)) for c in range(0, hidden, 256)]

    def kernel(
        w_hbm, x_hbm, t_hbm, f_hbm, grown, bases_ref, rights_ref,
        f, w, x, t, first, sums, gram_x,
        part0, part1, rs0, rs1, own0, own1, p_own, p0_in, p_out, p_in, v12, c_out, c_in, q_out, q_in,
        load_sem, rs_send, rs_recv, ag_send, ag_recv, x_send, x_recv,
    ):
        r, s = lax.axis_index("replica"), lax.axis_index("shard")

        def peer(dr, ds):
            return (lax.rem(r + (dr + replicas), replicas), lax.rem(s + ds, shards))

        def load(source, target, number):
            return pltpu.make_async_copy(source, target, load_sem.at[number])

        def send(source, target, send_sem, recv_sem, where):
            return pltpu.make_async_remote_copy(
                src_ref=source, dst_ref=target, send_sem=send_sem, recv_sem=recv_sem,
                device_id=where, device_id_type=MESH,
            )

        chunks = depth // CHUNK
        parts = [(c * CHUNK, CHUNK) for c in range(chunks - 1)]
        parts += [(depth - CHUNK, CHUNK // 2), (depth - CHUNK // 2, CHUNK // 2)]
        load_f, load_t = load(f_hbm, f, 0), load(t_hbm, t, 1)
        load_f.start()
        load_t.start()
        loads = []
        for number, (start, size) in enumerate(parts):
            span = pl.ds(start, size)
            loads.append(load(w_hbm.at[span], w.at[span], 2 + 2 * number))
            loads.append(load(x_hbm.at[:, span], x.at[:, span], 3 + 2 * number))
        for copy in loads:
            copy.start()

        barrier = pltpu.get_barrier_semaphore()
        friends = [(0, o) for o in range(1, shards)]
        friends += [(1, o) for o in range(shards)] + [(-1, o) for o in range(shards)]
        friends += [(2, 0), (-2, 0), (4, 0), (-4, 0), (6, 0), (-6, 0)]
        for dr, ds in friends:
            pl.semaphore_signal(barrier, inc=1, device_id=peer(dr, ds), device_id_type=MESH)

        c_out[...] = jnp.zeros_like(c_out)
        load_f.wait()
        shared = f[...].astype(BF16)
        load_t.wait()
        goal = mm(shared, t[...], NT)
        images, inside = [], -goal
        for number, (start, size) in enumerate(parts):
            loads[2 * number].wait()
            images.append(mm(shared, w[start : start + size, :], NT))
            loads[2 * number + 1].wait()
            inside = inside + mm(images[-1], x[:, start : start + size], NT)
        image = jnp.concatenate(images, axis=1) - 0.3 * mm(inside, x[...], NN)
        image, goal = image.astype(BF16), goal.astype(BF16)
        part0[:, :depth] = image[:RANK]
        part0[:, depth:] = goal[:RANK]
        part1[:, :depth] = image[RANK:]
        part1[:, depth:] = goal[RANK:]

        def piece(ref, index):
            return ref.at[:, pl.ds(pl.multiple_of(index * lanes, 128), lanes)]

        pl.semaphore_wait(barrier, len(friends))
        scatter0, scatter1 = [], []
        for o in range(1, shards):
            where = peer(0, o)
            scatter0.append(send(piece(part0, where[1]), rs0.at[o], rs_send.at[0, o], rs_recv.at[0, o], where))
            scatter0[-1].start()
        for o in range(1, shards):
            where = peer(0, o)
            scatter1.append(send(piece(part1, where[1]), rs1.at[o], rs_send.at[1, o], rs_recv.at[1, o], where))
            scatter1[-1].start()

        for c, width in blocks:
            product = mm(x[...], w[:, c : c + width], NN) - t[:, c : c + width].astype(F32)
            first[:, c : c + width] = product
            sums[0, :, c : c + width] = product.astype(BF16)

        for copy in scatter0:
            copy.wait_recv()
        total = piece(part0, s)[...].astype(F32)
        for o in range(1, shards):
            total = total + rs0[o].astype(F32)
        own0[...] = total.astype(BF16)
        piece(p_own, s)[...] = total.astype(BF16)
        gather0 = []
        for dr, o in [(0, o) for o in range(1, shards)] + [(1, o) for o in range(shards)]:
            target = piece(p_own if dr == 0 else p0_in, s)
            number = o if dr == 0 else shards + o
            gather0.append(send(own0, target, ag_send.at[number], ag_recv.at[number], peer(dr, o)))
            gather0[-1].start()
        for copy in scatter1:
            copy.wait_recv()
        total = piece(part1, s)[...].astype(F32)
        for o in range(1, shards):
            total = total + rs1[o].astype(F32)
        own1[...] = total.astype(BF16)
        piece(v12, s)[...] = total.astype(BF16)
        gather1 = []
        for o in range(1, shards):
            number = 2 * shards + o
            gather1.append(send(own1, piece(v12, s), ag_send.at[number], ag_recv.at[number], peer(0, o)))
            gather1[-1].start()

        for c in range(0, tokens, 256):
            gram_x[:, c : c + 256] = mm(x[...], x[c : c + 256, :], NT).astype(BF16)
        for step in (1, 2):
            for c, width in blocks:
                last = sums[step - 1, :, c : c + width]
                product = mm(gram_x[...], last, NN)
                value = first[:, c : c + width] + last.astype(F32) - 0.3 * product
                sums[step, :, c : c + width] = value.astype(BF16)

        def grow(c):
            rows = slice(c * CHUNK, (c + 1) * CHUNK)
            product = mm(x[:, rows], sums[2], TN)
            grown[rows, :] = (w[rows, :].astype(F32) - 0.3 * product).astype(BF16)

        def exchange(source, target, number, distance):
            copy = send(source, target, x_send.at[number], x_recv.at[number], peer(distance, 0))
            copy.start()
            return copy

        for copy in gather0:
            copy.wait_recv()
        basis0 = orthonormal(p_own[:, :depth].astype(F32) - p0_in[:, :depth].astype(F32))
        for copy in gather1:
            copy.wait_recv()
        image = v12[:, :depth]
        inner0 = mm(image, basis0, NT)
        c_out[0, :, :RANK] = inner0
        sent_c0 = exchange(c_out.at[0], c_in.at[0], 0, 1)
        inside = mm(jnp.concatenate([image, basis0], axis=0), x[...], NT)
        inside0 = inside[2 * RANK :]
        inside = jnp.concatenate([inside[: 2 * RANK] - v12[:, depth:].astype(F32), inside0], axis=0)
        change = 0.3 * mm(inside, x[...], NN)
        image = image.astype(F32) - change[: 2 * RANK]
        moved0 = basis0.astype(F32) - change[2 * RANK :]
        sent_c0.wait_recv()
        inner0 = inner0 - c_in[0, :, :RANK]
        image = image - 0.5 * mm(inner0, moved0, NN)
        left1 = image[:RANK]
        p_out[0] = left1.astype(BF16)
        sent_p1 = exchange(p_out.at[0], p_in.at[0], 1, 2)

        right0 = mm(basis0, w[...], NN) - 0.3 * mm(inside0, sums[0], NN)
        q_out[0] = right0.astype(BF16)
        sent_q0 = exchange(q_out.at[0], q_in.at[0], 2, 1)
        image = image[RANK:]
        inside = mm(jnp.concatenate([image, moved0], axis=0), x[...], NT)
        inside = jnp.concatenate([inside[:RANK] - v12[RANK:, depth:].astype(F32), inside[RANK:]], axis=0)
        change = 0.3 * mm(inside, x[...], NN)
        next_image = image - change[:RANK]
        p_out[1] = next_image.astype(BF16)
        sent_p2 = exchange(p_out.at[1], p_in.at[1], 3, 4)
        twice0 = moved0 - change[RANK:]
        grow(0)
        grow(1)

        sent_p1.wait_recv()
        basis1 = orthonormal(left1 - p_in[0].astype(F32))
        inner1 = mm(image, basis1, NT)
        c_out[1, :RANK, :RANK] = inner1
        sent_c1 = [
            exchange(c_out.at[1, pl.ds(0, RANK)], c_in.at[1 + n, pl.ds(0, RANK)], 4 + n, distance)
            for n, distance in enumerate((2, 4, 6))
        ]
        inside1 = mm(basis1, x[...], NT)
        moved1 = basis1.astype(F32) - 0.3 * mm(inside1, x[...], NN)
        p_out[2] = moved1.astype(BF16)
        sent_m1 = exchange(p_out.at[2], p_in.at[2], 7, 4)

        sent_q0.wait_recv()
        right0 = right0 - q_in[0].astype(F32)
        right1 = mm(basis1, w[...], NN) - 0.3 * mm(inside1, sums[1], NN)
        right1 = right1 - 0.5 * mm(mm(basis1, moved0, NT), right0, NN)
        q_out[1] = right1.astype(BF16)
        sent_q1 = exchange(q_out.at[1], q_in.at[1], 8, 2)
        for c in range(2, chunks):
            grow(c)
        bases_ref[:RANK, :] = twice0.astype(BF16)
        bases_ref[RANK : 2 * RANK, :] = moved1.astype(BF16)
        rights_ref[:RANK, :] = right0.astype(BF16)

        sent_p2.wait_recv()
        for copy in sent_c1:
            copy.wait_recv()
        inner = inner1 - c_in[1, :RANK, :RANK]
        left2 = next_image - 0.5 * mm(inner, moved1, NN)
        inner = c_in[2, :RANK, :RANK] - c_in[3, :RANK, :RANK]
        sent_q1.wait_recv()
        right1 = right1 - q_in[1].astype(F32)
        sent_m1.wait_recv()
        left2 = left2 - (p_in[1].astype(F32) - 0.5 * mm(inner, p_in[2], NN))
        inverse, pieces = factored(left2)
        raw = mm(pieces, grown[...], NN)
        raw = raw - 0.5 * mm(mm(pieces, twice0, NT), right0, NN) - 0.5 * mm(mm(pieces, moved1, NT), right1, NN)
        right2 = product_of(inverse, raw[:RANK] + raw[RANK:])
        q_out[2] = right2.astype(BF16)
        sent_q2 = exchange(q_out.at[2], q_in.at[2], 9, 4)
        basis2 = product_of(inverse, left2).astype(BF16)
        bases_ref[2 * RANK :, :] = basis2
        rights_ref[RANK : 2 * RANK, :] = right1.astype(BF16)
        started = scatter0 + scatter1 + gather0 + gather1
        for copy in started + sent_c1 + [sent_c0, sent_p1, sent_p2, sent_m1, sent_q0, sent_q1]:
            copy.wait_send()
        sent_q2.wait_recv()
        rights_ref[2 * RANK :, :] = (right2 - q_in[2].astype(F32)).astype(BF16)
        sent_q2.wait_send()

    vm, dma = pltpu.VMEM, pltpu.SemaphoreType.DMA
    scratch = [
        vm((3 * RANK, hidden), F32), vm((depth, hidden), BF16), vm((tokens, depth), BF16), vm((tokens, hidden), BF16),
        vm((tokens, hidden), F32), vm((3, tokens, hidden), BF16), vm((tokens, tokens), BF16),
        vm((RANK, wide), BF16), vm((2 * RANK, wide), BF16),
        vm((shards, RANK, lanes), BF16), vm((shards, 2 * RANK, lanes), BF16),
        vm((RANK, lanes), BF16), vm((2 * RANK, lanes), BF16),
        vm((RANK, wide), BF16), vm((RANK, wide), BF16), vm((3, RANK, depth), BF16), vm((3, RANK, depth), BF16),
        vm((2 * RANK, wide), BF16),
        vm((2, 2 * RANK, 128), F32), vm((4, 2 * RANK, 128), F32),
        vm((3, RANK, hidden), BF16), vm((3, RANK, hidden), BF16),
        dma((2 * depth // CHUNK + 4,)), dma((2, shards)), dma((2, shards)),
        dma((3 * shards,)), dma((3 * shards,)), dma((10,)), dma((10,)),
    ]
    return kernel, scratch


def solution(mesh):
    replicas, shards = mesh.shape["replica"], mesh.shape["shard"]

    def per_device(weights, x, targets, factors):
        weight = weights[0]
        depth, hidden = weight.shape
        tokens = x.shape[0]
        shared = factors.transpose(0, 2, 1).reshape(3 * RANK, hidden)
        kernel, scratch = make_kernel(replicas, shards, depth, hidden, tokens)
        in_vmem = pl.BlockSpec(memory_space=pltpu.VMEM)
        grown, bases, rights = pl.pallas_call(
            kernel,
            out_shape=(
                pltpu.VMEM((depth, hidden), BF16),
                jax.ShapeDtypeStruct((3 * RANK, depth), BF16),
                jax.ShapeDtypeStruct((3 * RANK, hidden), BF16),
            ),
            in_specs=[pl.BlockSpec(memory_space=pltpu.HBM)] * 4,
            out_specs=(in_vmem, in_vmem, in_vmem),
            scratch_shapes=scratch,
            compiler_params=pltpu.CompilerParams(
                collective_id=0, has_side_effects=True, vmem_limit_bytes=40 * 2**20
            ),
            name="rounds",
        )(*(pltpu.with_memory_space_constraint(v, pltpu.HBM) for v in (weight, x, targets, shared)))
        return pl.pallas_call(
            update_kernel,
            out_shape=jax.ShapeDtypeStruct((depth, hidden), BF16),
            in_specs=[in_vmem] * 3,
            out_specs=pl.BlockSpec(memory_space=pltpu.HBM),
            scratch_shapes=[pltpu.VMEM((depth, hidden), BF16), pltpu.SemaphoreType.DMA((pl.cdiv(hidden, 256),))],
            compiler_params=pltpu.CompilerParams(vmem_limit_bytes=16 * 2**20),
            name="update",
        )(grown, bases, rights)[None]

    in_specs = (
        P("replica", None, "shard"),
        P("replica", None),
        P("replica", "shard"),
        P(None, "shard", None),
    )
    return jax.shard_map(
        per_device, mesh=mesh, in_specs=in_specs, out_specs=P("replica", None, "shard"), check_vma=False
    )
```

```python
import jax
import jax.numpy as jnp
from jax import lax
from jax.experimental import pallas as pl
from jax.experimental.pallas import tpu as pltpu
from jax.sharding import PartitionSpec as P

RANK = 16
F32, BF16 = jnp.float32, jnp.bfloat16
NT = (((1,), (1,)), ((), ()))
NN = (((1,), (0,)), ((), ()))
TN = (((0,), (0,)), ((), ()))
MESH = pl.DeviceIdType.MESH
CHUNK = 512


def mm(a, b, dims):
    return lax.dot_general(a.astype(BF16), b.astype(BF16), dims, preferred_element_type=F32)


def inverse_factor(gram):
    shape = (RANK, 128)
    lane = lax.broadcasted_iota(jnp.int32, shape, 1)
    row = lax.broadcasted_iota(jnp.int32, shape, 0)
    inverse = jnp.where(lane == row, 1.0, 0.0).astype(F32)
    columns = [jnp.broadcast_to(gram[:, k : k + 1], shape) for k in range(RANK)]
    pivots = jnp.ones(shape, F32)
    for j in range(RANK):
        pivot = jnp.broadcast_to(columns[j][j : j + 1, :], shape)
        pivots = jnp.where(row == j, pivot, pivots)
        if j < RANK - 1:
            factor = jnp.where(row > j, columns[j] / pivot, 0.0)
            for k in range(j + 1, RANK):
                columns[k] = columns[k] - factor * jnp.broadcast_to(columns[k][j : j + 1, :], shape)
            inverse = inverse - factor * jnp.broadcast_to(inverse[j : j + 1, :], shape)
    return (lax.rsqrt(pivots) * inverse)[:, :RANK]


def product_of(inverse, value):
    high = value.astype(BF16)
    rest = (value - high.astype(F32)).astype(BF16)
    result = mm(inverse, high, NN) + mm(inverse, rest, NN)
    return result[:RANK] + result[RANK:]


def factored(diff):
    high = diff.astype(BF16)
    rest = diff - high.astype(F32)
    middle = rest.astype(BF16)
    low = (rest - middle.astype(F32)).astype(BF16)
    pieces = jnp.concatenate([high, middle, low], axis=0)
    gram = lax.dot_general(pieces, pieces, NT, preferred_element_type=F32)
    gram = gram[:RANK] + gram[RANK : 2 * RANK] + gram[2 * RANK :]
    gram = gram[:, :RANK] + gram[:, RANK : 2 * RANK] + gram[:, 2 * RANK :]
    inverse = inverse_factor(gram)
    top = inverse.astype(BF16)
    inverse = jnp.concatenate([top, (inverse - top.astype(F32)).astype(BF16)], axis=0)
    return inverse, pieces[: 2 * RANK]


def orthonormal(diff):
    inverse, _ = factored(diff)
    return product_of(inverse, diff).astype(BF16)


def update_kernel(grown, bases, rights, out_hbm, staged, sem):
    for c in range(0, grown.shape[1], 256):
        columns = pl.ds(c, min(256, grown.shape[1] - c))
        delta = mm(bases[...], rights[:, columns], TN)
        staged[:, columns] = (grown[:, columns].astype(F32) - 0.5 * delta).astype(BF16)
    copy = pltpu.make_async_copy(staged, out_hbm, sem)
    copy.start()
    copy.wait()


def make_kernel(replicas, shards, depth, hidden, tokens):
    wide = depth + tokens
    lanes = wide // shards
    blocks = [(c, min(256, hidden - c)) for c in range(0, hidden, 256)]

    def kernel(
        w_hbm, x_hbm, t_hbm, f_hbm, grown, bases_ref, rights_ref,
        f, w, x, t, first, sums, gram_x,
        part0, part1, rs0, rs1, own0, own1, p_own, p0_in, p_out, p_in, v12, c_out, c_in, q_out, q_in,
        load_sem, rs_send, rs_recv, ag_send, ag_recv, x_send, x_recv,
    ):
        r, s = lax.axis_index("replica"), lax.axis_index("shard")

        def peer(dr, ds):
            return (lax.rem(r + (dr + replicas), replicas), lax.rem(s + ds, shards))

        def load(source, target, number):
            return pltpu.make_async_copy(source, target, load_sem.at[number])

        def send(source, target, send_sem, recv_sem, where):
            return pltpu.make_async_remote_copy(
                src_ref=source, dst_ref=target, send_sem=send_sem, recv_sem=recv_sem,
                device_id=where, device_id_type=MESH,
            )

        chunks = depth // CHUNK
        halves = [(0, tokens // 2), (tokens // 2, tokens // 2)]
        load_f = load(f_hbm, f, 0)
        load_w = [
            load(w_hbm.at[pl.ds(c * CHUNK, CHUNK)], w.at[pl.ds(c * CHUNK, CHUNK)], 4 + c)
            for c in range(chunks)
        ]
        load_t = load(t_hbm, t, 1)
        load_x = [load(x_hbm.at[pl.ds(*half)], x.at[pl.ds(*half)], 2 + n) for n, half in enumerate(halves)]
        for copy in [load_f] + load_w + [load_t] + load_x:
            copy.start()

        barrier = pltpu.get_barrier_semaphore()
        friends = [(0, o) for o in range(1, shards)]
        friends += [(1, o) for o in range(shards)] + [(-1, o) for o in range(shards)]
        friends += [(2, 0), (-2, 0), (4, 0), (-4, 0), (6, 0), (-6, 0), (3, 0), (-3, 0)]
        for dr, ds in friends:
            pl.semaphore_signal(barrier, inc=1, device_id=peer(dr, ds), device_id_type=MESH)

        c_out[...] = jnp.zeros_like(c_out)
        load_f.wait()
        shared = f[...].astype(BF16)
        images = []
        for c in range(chunks):
            load_w[c].wait()
            images.append(mm(shared, w[c * CHUNK : (c + 1) * CHUNK, :], NT))
        image = jnp.concatenate(images, axis=1)
        load_t.wait()
        goal = mm(shared, t[...], NT)
        change = jnp.zeros_like(image)
        for n, (start, size) in enumerate(halves):
            load_x[n].wait()
            rows = slice(start, start + size)
            inside = mm(image, x[rows, :], NT) - goal[:, rows]
            change = change + mm(inside, x[rows, :], NN)
        image = image - 0.3 * change
        image, goal = image.astype(BF16), goal.astype(BF16)
        part0[:, :depth] = image[:RANK]
        part0[:, depth:] = goal[:RANK]
        part1[:, :depth] = image[RANK:]
        part1[:, depth:] = goal[RANK:]

        def piece(ref, index):
            return ref.at[:, pl.ds(pl.multiple_of(index * lanes, 128), lanes)]

        pl.semaphore_wait(barrier, len(friends))
        scatter0, scatter1 = [], []
        for o in range(1, shards):
            where = peer(0, o)
            scatter0.append(send(piece(part0, where[1]), rs0.at[o], rs_send.at[0, o], rs_recv.at[0, o], where))
            scatter0[-1].start()
        for o in range(1, shards):
            where = peer(0, o)
            scatter1.append(send(piece(part1, where[1]), rs1.at[o], rs_send.at[1, o], rs_recv.at[1, o], where))
            scatter1[-1].start()

        for c, width in blocks:
            product = mm(x[...], w[:, c : c + width], NN) - t[:, c : c + width].astype(F32)
            first[:, c : c + width] = product
            sums[0, :, c : c + width] = product.astype(BF16)

        for copy in scatter0:
            copy.wait_recv()
        total = piece(part0, s)[...].astype(F32)
        for o in range(1, shards):
            total = total + rs0[o].astype(F32)
        own0[...] = total.astype(BF16)
        piece(p_own, s)[...] = total.astype(BF16)
        gather0 = []
        for dr, o in [(0, o) for o in range(1, shards)] + [(1, o) for o in range(shards)]:
            target = piece(p_own if dr == 0 else p0_in, s)
            number = o if dr == 0 else shards + o
            gather0.append(send(own0, target, ag_send.at[number], ag_recv.at[number], peer(dr, o)))
            gather0[-1].start()
        for copy in scatter1:
            copy.wait_recv()
        total = piece(part1, s)[...].astype(F32)
        for o in range(1, shards):
            total = total + rs1[o].astype(F32)
        own1[...] = total.astype(BF16)
        piece(v12, s)[...] = total.astype(BF16)
        gather1 = []
        for o in range(1, shards):
            number = 2 * shards + o
            gather1.append(send(own1, piece(v12, s), ag_send.at[number], ag_recv.at[number], peer(0, o)))
            gather1[-1].start()

        for c in range(0, tokens, 256):
            gram_x[:, c : c + 256] = mm(x[...], x[c : c + 256, :], NT).astype(BF16)
        for step in (1, 2):
            for c, width in blocks:
                last = sums[step - 1, :, c : c + width]
                product = mm(gram_x[...], last, NN)
                value = first[:, c : c + width] + last.astype(F32) - 0.3 * product
                sums[step, :, c : c + width] = value.astype(BF16)

        def grow(c):
            rows = slice(c * CHUNK, (c + 1) * CHUNK)
            product = mm(x[:, rows], sums[2], TN)
            grown[rows, :] = (w[rows, :].astype(F32) - 0.3 * product).astype(BF16)

        def exchange(source, target, number, distance):
            copy = send(source, target, x_send.at[number], x_recv.at[number], peer(distance, 0))
            copy.start()
            return copy

        for copy in gather0:
            copy.wait_recv()
        basis0 = orthonormal(p_own[:, :depth].astype(F32) - p0_in[:, :depth].astype(F32))
        for copy in gather1:
            copy.wait_recv()
        image = v12[:, :depth]
        inner0 = mm(image, basis0, NT)
        c_out[0, :, :RANK] = inner0
        sent_c0 = [exchange(c_out.at[0], c_in.at[n], n, n + 1) for n in range(3)]
        inside = mm(jnp.concatenate([image, basis0], axis=0), x[...], NT)
        inside0 = inside[2 * RANK :]
        inside = jnp.concatenate([inside[: 2 * RANK] - v12[:, depth:].astype(F32), inside0], axis=0)
        change = 0.3 * mm(inside, x[...], NN)
        image = image.astype(F32) - change[: 2 * RANK]
        moved0 = basis0.astype(F32) - change[2 * RANK :]
        p_out[0] = image[:RANK].astype(BF16)
        p_out[1] = moved0.astype(BF16)
        sent_p1 = exchange(p_out.at[0], p_in.at[0], 3, 2)
        sent_m0 = exchange(p_out.at[1], p_in.at[1], 4, 2)

        inside = mm(jnp.concatenate([image[RANK:], moved0], axis=0), x[...], NT)
        inside = jnp.concatenate([inside[:RANK] - v12[RANK:, depth:].astype(F32), inside[RANK:]], axis=0)
        change = 0.3 * mm(inside, x[...], NN)
        next_image = image[RANK:] - change[:RANK]
        twice0 = moved0 - change[RANK:]
        right0 = mm(basis0, w[...], NN) - 0.3 * mm(inside0, sums[0], NN)
        q_out[0] = right0.astype(BF16)
        sent_q0 = exchange(q_out.at[0], q_in.at[0], 5, 1)
        grow(0)
        grow(1)

        for copy in sent_c0:
            copy.wait_recv()
        inner = inner0 - c_in[0, :, :RANK]
        other = c_in[1, :RANK, :RANK] - c_in[2, :RANK, :RANK]
        next_image = next_image - 0.5 * mm(inner[RANK:], twice0, NN)
        p_out[2] = next_image.astype(BF16)
        sent_p2 = exchange(p_out.at[2], p_in.at[2], 6, 4)
        image = image - 0.5 * mm(inner, moved0, NN)
        left1, image = image[:RANK], image[RANK:]
        sent_p1.wait_recv()
        sent_m0.wait_recv()
        basis1 = orthonormal(left1 - (p_in[0].astype(F32) - 0.5 * mm(other, p_in[1], NN)))
        inner1 = mm(image, basis1, NT)
        c_out[1, :RANK, :RANK] = inner1
        sent_c1 = [
            exchange(c_out.at[1, pl.ds(0, RANK)], c_in.at[3 + n, pl.ds(0, RANK)], 7 + n, distance)
            for n, distance in enumerate((2, 4, 6))
        ]
        inside1 = mm(basis1, x[...], NT)
        moved1 = basis1.astype(F32) - 0.3 * mm(inside1, x[...], NN)
        p_out[3] = moved1.astype(BF16)
        sent_m1 = exchange(p_out.at[3], p_in.at[3], 10, 4)

        sent_q0.wait_recv()
        right0 = right0 - q_in[0].astype(F32)
        right1 = mm(basis1, w[...], NN) - 0.3 * mm(inside1, sums[1], NN)
        right1 = right1 - 0.5 * mm(mm(basis1, moved0, NT), right0, NN)
        q_out[1] = right1.astype(BF16)
        sent_q1 = exchange(q_out.at[1], q_in.at[1], 11, 2)
        for c in range(2, chunks):
            grow(c)
        bases_ref[:RANK, :] = twice0.astype(BF16)
        bases_ref[RANK : 2 * RANK, :] = moved1.astype(BF16)
        rights_ref[:RANK, :] = right0.astype(BF16)

        sent_p2.wait_recv()
        for copy in sent_c1:
            copy.wait_recv()
        inner = inner1 - c_in[3, :RANK, :RANK]
        left2 = next_image - 0.5 * mm(inner, moved1, NN)
        other = c_in[4, :RANK, :RANK] - c_in[5, :RANK, :RANK]
        sent_q1.wait_recv()
        right1 = right1 - q_in[1].astype(F32)
        sent_m1.wait_recv()
        left2 = left2 - (p_in[2].astype(F32) - 0.5 * mm(other, p_in[3], NN))
        inverse, pieces = factored(left2)
        raw = mm(pieces, grown[...], NN)
        raw = raw - 0.5 * mm(mm(pieces, twice0, NT), right0, NN) - 0.5 * mm(mm(pieces, moved1, NT), right1, NN)
        raw = raw[:RANK] + raw[RANK:]
        q_out[2] = raw.astype(BF16)
        sent_q2 = exchange(q_out.at[2], q_in.at[2], 12, 4)
        c_out[2, :RANK, :RANK] = inverse[:RANK].astype(F32) + inverse[RANK:].astype(F32)
        sent_i2 = exchange(c_out.at[2, pl.ds(0, RANK)], c_in.at[6, pl.ds(0, RANK)], 13, 4)
        right2 = product_of(inverse, raw)
        basis2 = product_of(inverse, left2).astype(BF16)
        bases_ref[2 * RANK :, :] = basis2
        rights_ref[RANK : 2 * RANK, :] = right1.astype(BF16)
        started = scatter0 + scatter1 + gather0 + gather1
        for copy in started + sent_c0 + sent_c1 + [sent_p1, sent_p2, sent_m0, sent_m1, sent_q0, sent_q1]:
            copy.wait_send()
        sent_i2.wait_recv()
        inverse = c_in[6, :RANK, :RANK]
        top = inverse.astype(BF16)
        inverse = jnp.concatenate([top, (inverse - top.astype(F32)).astype(BF16)], axis=0)
        sent_q2.wait_recv()
        other = mm(inverse, q_in[2], NN)
        rights_ref[2 * RANK :, :] = (right2 - other[:RANK] - other[RANK:]).astype(BF16)
        sent_i2.wait_send()
        sent_q2.wait_send()

    vm, dma = pltpu.VMEM, pltpu.SemaphoreType.DMA
    scratch = [
        vm((3 * RANK, hidden), F32), vm((depth, hidden), BF16), vm((tokens, depth), BF16), vm((tokens, hidden), BF16),
        vm((tokens, hidden), F32), vm((3, tokens, hidden), BF16), vm((tokens, tokens), BF16),
        vm((RANK, wide), BF16), vm((2 * RANK, wide), BF16),
        vm((shards, RANK, lanes), BF16), vm((shards, 2 * RANK, lanes), BF16),
        vm((RANK, lanes), BF16), vm((2 * RANK, lanes), BF16),
        vm((RANK, wide), BF16), vm((RANK, wide), BF16), vm((4, RANK, depth), BF16), vm((4, RANK, depth), BF16),
        vm((2 * RANK, wide), BF16),
        vm((3, 2 * RANK, 128), F32), vm((7, 2 * RANK, 128), F32),
        vm((3, RANK, hidden), BF16), vm((3, RANK, hidden), BF16),
        dma((depth // CHUNK + 4,)), dma((2, shards)), dma((2, shards)),
        dma((3 * shards,)), dma((3 * shards,)), dma((14,)), dma((14,)),
    ]
    return kernel, scratch


def solution(mesh):
    replicas, shards = mesh.shape["replica"], mesh.shape["shard"]

    def per_device(weights, x, targets, factors):
        weight = weights[0]
        depth, hidden = weight.shape
        tokens = x.shape[0]
        shared = factors.transpose(0, 2, 1).reshape(3 * RANK, hidden)
        kernel, scratch = make_kernel(replicas, shards, depth, hidden, tokens)
        in_vmem = pl.BlockSpec(memory_space=pltpu.VMEM)
        grown, bases, rights = pl.pallas_call(
            kernel,
            out_shape=(
                pltpu.VMEM((depth, hidden), BF16),
                jax.ShapeDtypeStruct((3 * RANK, depth), BF16),
                jax.ShapeDtypeStruct((3 * RANK, hidden), BF16),
            ),
            in_specs=[pl.BlockSpec(memory_space=pltpu.HBM)] * 4,
            out_specs=(in_vmem, in_vmem, in_vmem),
            scratch_shapes=scratch,
            compiler_params=pltpu.CompilerParams(
                collective_id=0, has_side_effects=True, vmem_limit_bytes=40 * 2**20
            ),
            name="rounds",
        )(*(pltpu.with_memory_space_constraint(v, pltpu.HBM) for v in (weight, x, targets, shared)))
        return pl.pallas_call(
            update_kernel,
            out_shape=jax.ShapeDtypeStruct((depth, hidden), BF16),
            in_specs=[in_vmem] * 3,
            out_specs=pl.BlockSpec(memory_space=pltpu.HBM),
            scratch_shapes=[pltpu.VMEM((depth, hidden), BF16), pltpu.SemaphoreType.DMA],
            compiler_params=pltpu.CompilerParams(vmem_limit_bytes=16 * 2**20),
            name="update",
        )(grown, bases, rights)[None]

    in_specs = (
        P("replica", None, "shard"),
        P("replica", None),
        P("replica", "shard"),
        P(None, "shard", None),
    )
    return jax.shard_map(
        per_device, mesh=mesh, in_specs=in_specs, out_specs=P("replica", None, "shard"), check_vma=False
    )
```

```python
import jax
import jax.numpy as jnp
from jax import lax
from jax.experimental import pallas as pl
from jax.experimental.pallas import tpu as pltpu
from jax.sharding import PartitionSpec as P

RANK = 16
F32, BF16 = jnp.float32, jnp.bfloat16
NT = (((1,), (1,)), ((), ()))
NN = (((1,), (0,)), ((), ()))
TN = (((0,), (0,)), ((), ()))
MESH = pl.DeviceIdType.MESH
CHUNK = 512


def mm(a, b, dims):
    return lax.dot_general(a.astype(BF16), b.astype(BF16), dims, preferred_element_type=F32)


def inverse_factor(gram):
    shape = (RANK, 128)
    lane = lax.broadcasted_iota(jnp.int32, shape, 1)
    row = lax.broadcasted_iota(jnp.int32, shape, 0)
    inverse = jnp.where(lane == row, 1.0, 0.0).astype(F32)
    columns = [jnp.broadcast_to(gram[:, k : k + 1], shape) for k in range(RANK)]
    pivots = jnp.ones(shape, F32)
    for j in range(RANK):
        pivot = jnp.broadcast_to(columns[j][j : j + 1, :], shape)
        pivots = jnp.where(row == j, pivot, pivots)
        if j < RANK - 1:
            factor = jnp.where(row > j, columns[j] / pivot, 0.0)
            for k in range(j + 1, RANK):
                columns[k] = columns[k] - factor * jnp.broadcast_to(columns[k][j : j + 1, :], shape)
            inverse = inverse - factor * jnp.broadcast_to(inverse[j : j + 1, :], shape)
    return (lax.rsqrt(pivots) * inverse)[:, :RANK]


def product_of(inverse, value):
    high = value.astype(BF16)
    rest = (value - high.astype(F32)).astype(BF16)
    result = mm(inverse, high, NN) + mm(inverse, rest, NN)
    return result[:RANK] + result[RANK:]


def factored(diff):
    high = diff.astype(BF16)
    rest = diff - high.astype(F32)
    middle = rest.astype(BF16)
    low = (rest - middle.astype(F32)).astype(BF16)
    pieces = jnp.concatenate([high, middle, low], axis=0)
    gram = lax.dot_general(pieces, pieces, NT, preferred_element_type=F32)
    gram = gram[:RANK] + gram[RANK : 2 * RANK] + gram[2 * RANK :]
    gram = gram[:, :RANK] + gram[:, RANK : 2 * RANK] + gram[:, 2 * RANK :]
    inverse = inverse_factor(gram)
    top = inverse.astype(BF16)
    inverse = jnp.concatenate([top, (inverse - top.astype(F32)).astype(BF16)], axis=0)
    return inverse, pieces[: 2 * RANK]


def orthonormal(diff):
    inverse, _ = factored(diff)
    return product_of(inverse, diff).astype(BF16)


def update_kernel(grown, bases, rights, out_hbm, staged, sem):
    depth, hidden = grown.shape
    edges = [0, *range(256, depth, 512), depth]
    copies = []
    for number, (start, stop) in enumerate(zip(edges, edges[1:])):
        rows = slice(start, stop)
        for c in range(0, hidden, 256):
            columns = slice(c, min(c + 256, hidden))
            delta = mm(bases[rows, :], rights[:, columns], NN)
            staged[rows, columns] = (grown[rows, columns].astype(F32) - delta).astype(BF16)
        span = pl.ds(start, stop - start)
        copies.append(pltpu.make_async_copy(staged.at[span], out_hbm.at[span], sem.at[number]))
        copies[-1].start()
    for copy in copies:
        copy.wait()


def make_kernel(replicas, shards, depth, hidden, tokens):
    wide = depth + tokens
    lanes = wide // shards
    blocks = [(c, min(256, hidden - c)) for c in range(0, hidden, 256)]

    def kernel(
        w_hbm, x_hbm, t_hbm, f_hbm, grown, bases_ref, rights_ref,
        f, w, x, xt, t, first, sums, gram_x,
        part0, part1, rs0, rs1, own0, own1, p_own, p0_in, p_out, p_in, v12, c_out, c_in, q_out, q_in,
        load_sem, rs_send, rs_recv, ag_send, ag_recv, x_send, x_recv,
    ):
        r, s = lax.axis_index("replica"), lax.axis_index("shard")

        def peer(dr, ds):
            return (lax.rem(r + (dr + replicas), replicas), lax.rem(s + ds, shards))

        def load(source, target, number):
            return pltpu.make_async_copy(source, target, load_sem.at[number])

        def send(source, target, send_sem, recv_sem, where):
            return pltpu.make_async_remote_copy(
                src_ref=source, dst_ref=target, send_sem=send_sem, recv_sem=recv_sem,
                device_id=where, device_id_type=MESH,
            )

        chunks = depth // CHUNK
        load_f, load_t, load_x = load(f_hbm, f, 0), load(t_hbm, t, 1), load(x_hbm, x, 2)
        load_w = [
            load(w_hbm.at[pl.ds(c * CHUNK, CHUNK)], w.at[pl.ds(c * CHUNK, CHUNK)], 3 + c)
            for c in range(chunks)
        ]
        for copy in [load_f] + load_w + [load_t, load_x]:
            copy.start()

        barrier = pltpu.get_barrier_semaphore()
        friends = [(0, o) for o in range(1, shards)]
        friends += [(1, o) for o in range(shards)] + [(-1, o) for o in range(shards)]
        friends += [(2, 0), (-2, 0), (4, 0), (-4, 0), (6, 0), (-6, 0)]
        for dr, ds in friends:
            pl.semaphore_signal(barrier, inc=1, device_id=peer(dr, ds), device_id_type=MESH)

        c_out[...] = jnp.zeros_like(c_out)
        load_f.wait()
        shared = f[...].astype(BF16)
        images = []
        for c in range(chunks):
            load_w[c].wait()
            images.append(mm(shared, w[c * CHUNK : (c + 1) * CHUNK, :], NT))
        load_t.wait()
        goal = mm(shared, t[...], NT)
        load_x.wait()
        image = jnp.concatenate(images, axis=1)
        image = image - 0.3 * mm(mm(image, x[...], NT) - goal, x[...], NN)
        image, goal = image.astype(BF16), goal.astype(BF16)
        part0[:, :depth] = image[:RANK]
        part0[:, depth:] = goal[:RANK]
        part1[:, :depth] = image[RANK:]
        part1[:, depth:] = goal[RANK:]

        def piece(ref, index):
            return ref.at[:, pl.ds(pl.multiple_of(index * lanes, 128), lanes)]

        pl.semaphore_wait(barrier, len(friends))
        scatter0, scatter1 = [], []
        for o in range(1, shards):
            where = peer(0, o)
            scatter0.append(send(piece(part0, where[1]), rs0.at[o], rs_send.at[0, o], rs_recv.at[0, o], where))
            scatter0[-1].start()
        for o in range(1, shards):
            where = peer(0, o)
            scatter1.append(send(piece(part1, where[1]), rs1.at[o], rs_send.at[1, o], rs_recv.at[1, o], where))
            scatter1[-1].start()

        for c, width in blocks:
            product = mm(x[...], w[:, c : c + width], NN) - t[:, c : c + width].astype(F32)
            first[:, c : c + width] = product
            sums[0, :, c : c + width] = product.astype(BF16)

        for copy in scatter0:
            copy.wait_recv()
        total = piece(part0, s)[...].astype(F32)
        for o in range(1, shards):
            total = total + rs0[o].astype(F32)
        own0[...] = total.astype(BF16)
        piece(p_own, s)[...] = total.astype(BF16)
        gather0 = []
        for dr, o in [(0, o) for o in range(1, shards)] + [(1, o) for o in range(shards)]:
            target = piece(p_own if dr == 0 else p0_in, s)
            number = o if dr == 0 else shards + o
            gather0.append(send(own0, target, ag_send.at[number], ag_recv.at[number], peer(dr, o)))
            gather0[-1].start()
        for copy in scatter1:
            copy.wait_recv()
        total = piece(part1, s)[...].astype(F32)
        for o in range(1, shards):
            total = total + rs1[o].astype(F32)
        own1[...] = total.astype(BF16)
        piece(v12, s)[...] = total.astype(BF16)
        gather1 = []
        for o in range(1, shards):
            number = 2 * shards + o
            gather1.append(send(own1, piece(v12, s), ag_send.at[number], ag_recv.at[number], peer(0, o)))
            gather1[-1].start()

        for c in range(chunks):
            xt[c * CHUNK : (c + 1) * CHUNK, :] = x[:, c * CHUNK : (c + 1) * CHUNK].T
        for c in range(0, tokens, 256):
            gram_x[:, c : c + 256] = mm(x[...], xt[:, c : c + 256], NN).astype(BF16)

        def next_sum(step):
            for c, width in blocks:
                last = sums[step - 1, :, c : c + width]
                product = mm(gram_x[...], last, NN)
                value = first[:, c : c + width] + last.astype(F32) - 0.3 * product
                sums[step, :, c : c + width] = value.astype(BF16)


        def grow(c):
            rows = slice(c * CHUNK, (c + 1) * CHUNK)
            product = mm(xt[rows, :], sums[2], NN)
            grown[rows, :] = (w[rows, :].astype(F32) - 0.3 * product).astype(BF16)

        def exchange(source, target, number, distance):
            copy = send(source, target, x_send.at[number], x_recv.at[number], peer(distance, 0))
            copy.start()
            return copy

        for copy in gather0:
            copy.wait_recv()
        basis0 = orthonormal(p_own[:, :depth].astype(F32) - p0_in[:, :depth].astype(F32))
        for copy in gather1:
            copy.wait_recv()
        image = v12[:, :depth]
        inner0 = mm(image, basis0, NT)
        c_out[0, :, :RANK] = inner0
        sent_c0 = exchange(c_out.at[0], c_in.at[0], 0, 1)
        inside = mm(jnp.concatenate([image, basis0], axis=0), xt[...], NN)
        inside0 = inside[2 * RANK :]
        inside = jnp.concatenate([inside[: 2 * RANK] - v12[:, depth:].astype(F32), inside0], axis=0)
        change = 0.3 * mm(inside, x[...], NN)
        image = image.astype(F32) - change[: 2 * RANK]
        moved0 = basis0.astype(F32) - change[2 * RANK :]
        next_sum(1)
        sent_c0.wait_recv()
        inner0 = inner0 - c_in[0, :, :RANK]
        image = image - 0.5 * mm(inner0, moved0, NN)
        left1 = image[:RANK]
        p_out[0] = left1.astype(BF16)
        sent_p1 = exchange(p_out.at[0], p_in.at[0], 1, 2)

        right0 = mm(basis0, w[...], NN) - 0.3 * mm(inside0, sums[0], NN)
        q_out[0] = right0.astype(BF16)
        sent_q0 = exchange(q_out.at[0], q_in.at[0], 2, 1)
        image = image[RANK:]
        inside = mm(jnp.concatenate([image, moved0], axis=0), xt[...], NN)
        inside = jnp.concatenate([inside[:RANK] - v12[RANK:, depth:].astype(F32), inside[RANK:]], axis=0)
        change = 0.3 * mm(inside, x[...], NN)
        next_image = image - change[:RANK]
        p_out[1] = next_image.astype(BF16)
        twice0 = moved0 - change[RANK:]
        next_sum(2)
        grow(0)

        sent_p1.wait_recv()
        sent_p2 = exchange(p_out.at[1], p_in.at[1], 3, 4)
        basis1 = orthonormal(left1 - p_in[0].astype(F32))
        inner1 = mm(image, basis1, NT)
        c_out[1, :RANK, :RANK] = inner1
        sent_c1 = [
            exchange(c_out.at[1, pl.ds(0, RANK)], c_in.at[1 + n, pl.ds(0, RANK)], 4 + n, distance)
            for n, distance in enumerate((2, 4, 6))
        ]
        inside1 = mm(basis1, xt[...], NN)
        moved1 = basis1.astype(F32) - 0.3 * mm(inside1, x[...], NN)
        p_out[2] = moved1.astype(BF16)
        sent_m1 = exchange(p_out.at[2], p_in.at[2], 7, 4)

        sent_q0.wait_recv()
        right0 = right0 - q_in[0].astype(F32)
        right1 = mm(basis1, w[...], NN) - 0.3 * mm(inside1, sums[1], NN)
        right1 = right1 - 0.5 * mm(mm(basis1, moved0, NT), right0, NN)
        q_out[1] = right1.astype(BF16)
        sent_q1 = exchange(q_out.at[1], q_in.at[1], 8, 2)
        for c in range(1, chunks):
            grow(c)

        sent_p2.wait_recv()
        for copy in sent_c1:
            copy.wait_recv()
        inner = inner1 - c_in[1, :RANK, :RANK]
        left2 = next_image - 0.5 * mm(inner, moved1, NN)
        inner = c_in[2, :RANK, :RANK] - c_in[3, :RANK, :RANK]
        sent_q1.wait_recv()
        right1 = right1 - q_in[1].astype(F32)
        sent_m1.wait_recv()
        left2 = left2 - (p_in[1].astype(F32) - 0.5 * mm(inner, p_in[2], NN))
        inverse, pieces = factored(left2)
        raw = mm(pieces, grown[...], NN)
        raw = raw - 0.5 * mm(mm(pieces, twice0, NT), right0, NN) - 0.5 * mm(mm(pieces, moved1, NT), right1, NN)
        raw = raw[:RANK] + raw[RANK:]
        q_out[2] = raw.astype(BF16)
        sent_q2 = exchange(q_out.at[2], q_in.at[2], 9, 4)
        c_out[2, :RANK, :RANK] = inverse[:RANK].astype(F32) + inverse[RANK:].astype(F32)
        sent_i2 = exchange(c_out.at[2, pl.ds(0, RANK)], c_in.at[4, pl.ds(0, RANK)], 10, 4)
        right2 = product_of(inverse, raw)
        basis2 = product_of(inverse, left2)
        bases_ref[...] = jnp.concatenate([twice0, moved1, basis2], axis=0).astype(BF16).T
        rights_ref[:RANK, :] = (0.5 * right0).astype(BF16)
        rights_ref[RANK : 2 * RANK, :] = (0.5 * right1).astype(BF16)
        started = scatter0 + scatter1 + gather0 + gather1
        for copy in started + sent_c1 + [sent_c0, sent_p1, sent_p2, sent_m1, sent_q0, sent_q1]:
            copy.wait_send()
        sent_i2.wait_recv()
        inverse = c_in[4, :RANK, :RANK]
        top = inverse.astype(BF16)
        inverse = jnp.concatenate([top, (inverse - top.astype(F32)).astype(BF16)], axis=0)
        sent_q2.wait_recv()
        other = mm(inverse, q_in[2], NN)
        rights_ref[2 * RANK :, :] = (0.5 * (right2 - other[:RANK] - other[RANK:])).astype(BF16)
        sent_i2.wait_send()
        sent_q2.wait_send()

    vm, dma = pltpu.VMEM, pltpu.SemaphoreType.DMA
    scratch = [
        vm((3 * RANK, hidden), F32), vm((depth, hidden), BF16), vm((tokens, depth), BF16), vm((depth, tokens), BF16),
        vm((tokens, hidden), BF16),
        vm((tokens, hidden), F32), vm((3, tokens, hidden), BF16), vm((tokens, tokens), BF16),
        vm((RANK, wide), BF16), vm((2 * RANK, wide), BF16),
        vm((shards, RANK, lanes), BF16), vm((shards, 2 * RANK, lanes), BF16),
        vm((RANK, lanes), BF16), vm((2 * RANK, lanes), BF16),
        vm((RANK, wide), BF16), vm((RANK, wide), BF16), vm((3, RANK, depth), BF16), vm((3, RANK, depth), BF16),
        vm((2 * RANK, wide), BF16),
        vm((3, 2 * RANK, 128), F32), vm((5, 2 * RANK, 128), F32),
        vm((3, RANK, hidden), BF16), vm((3, RANK, hidden), BF16),
        dma((depth // CHUNK + 3,)), dma((2, shards)), dma((2, shards)),
        dma((3 * shards,)), dma((3 * shards,)), dma((11,)), dma((11,)),
    ]
    return kernel, scratch


def solution(mesh):
    replicas, shards = mesh.shape["replica"], mesh.shape["shard"]

    def per_device(weights, x, targets, factors):
        weight = weights[0]
        depth, hidden = weight.shape
        tokens = x.shape[0]
        shared = factors.transpose(0, 2, 1).reshape(3 * RANK, hidden)
        kernel, scratch = make_kernel(replicas, shards, depth, hidden, tokens)
        in_vmem = pl.BlockSpec(memory_space=pltpu.VMEM)
        grown, bases, rights = pl.pallas_call(
            kernel,
            out_shape=(
                pltpu.VMEM((depth, hidden), BF16),
                jax.ShapeDtypeStruct((depth, 3 * RANK), BF16),
                jax.ShapeDtypeStruct((3 * RANK, hidden), BF16),
            ),
            in_specs=[pl.BlockSpec(memory_space=pltpu.HBM)] * 4,
            out_specs=(in_vmem, in_vmem, in_vmem),
            scratch_shapes=scratch,
            compiler_params=pltpu.CompilerParams(
                collective_id=0, has_side_effects=True, vmem_limit_bytes=40 * 2**20
            ),
            name="rounds",
        )(*(pltpu.with_memory_space_constraint(v, pltpu.HBM) for v in (weight, x, targets, shared)))
        return pl.pallas_call(
            update_kernel,
            out_shape=jax.ShapeDtypeStruct((depth, hidden), BF16),
            in_specs=[in_vmem] * 3,
            out_specs=pl.BlockSpec(memory_space=pltpu.HBM),
            scratch_shapes=[pltpu.VMEM((depth, hidden), BF16), pltpu.SemaphoreType.DMA((depth // 512 + 1,))],
            compiler_params=pltpu.CompilerParams(vmem_limit_bytes=16 * 2**20),
            name="update",
        )(grown, bases, rights)[None]

    in_specs = (
        P("replica", None, "shard"),
        P("replica", None),
        P("replica", "shard"),
        P(None, "shard", None),
    )
    return jax.shard_map(
        per_device, mesh=mesh, in_specs=in_specs, out_specs=P("replica", None, "shard"), check_vma=False
    )
```

```python
import jax
import jax.numpy as jnp
from jax import lax
from jax.experimental import pallas as pl
from jax.experimental.pallas import tpu as pltpu
from jax.sharding import PartitionSpec as P

RANK = 16
F32, BF16 = jnp.float32, jnp.bfloat16
NT = (((1,), (1,)), ((), ()))
NN = (((1,), (0,)), ((), ()))
TN = (((0,), (0,)), ((), ()))
MESH = pl.DeviceIdType.MESH
CHUNK = 512


def mm(a, b, dims):
    return lax.dot_general(a.astype(BF16), b.astype(BF16), dims, preferred_element_type=F32)


def inverse_factor(gram):
    shape = (RANK, 128)
    lane = lax.broadcasted_iota(jnp.int32, shape, 1)
    row = lax.broadcasted_iota(jnp.int32, shape, 0)
    inverse = jnp.where(lane == row, 1.0, 0.0).astype(F32)
    columns = [jnp.broadcast_to(gram[:, k : k + 1], shape) for k in range(RANK)]
    pivots = jnp.ones(shape, F32)
    for j in range(RANK):
        pivot = jnp.broadcast_to(columns[j][j : j + 1, :], shape)
        pivots = jnp.where(row == j, pivot, pivots)
        if j < RANK - 1:
            factor = jnp.where(row > j, columns[j] / pivot, 0.0)
            for k in range(j + 1, RANK):
                columns[k] = columns[k] - factor * jnp.broadcast_to(columns[k][j : j + 1, :], shape)
            inverse = inverse - factor * jnp.broadcast_to(inverse[j : j + 1, :], shape)
    return (lax.rsqrt(pivots) * inverse)[:, :RANK]


def product_of(inverse, value):
    high = value.astype(BF16)
    rest = (value - high.astype(F32)).astype(BF16)
    result = mm(inverse, high, NN) + mm(inverse, rest, NN)
    return result[:RANK] + result[RANK:]


def factored(diff):
    high = diff.astype(BF16)
    rest = diff - high.astype(F32)
    middle = rest.astype(BF16)
    low = (rest - middle.astype(F32)).astype(BF16)
    pieces = jnp.concatenate([high, middle, low], axis=0)
    gram = lax.dot_general(pieces, pieces, NT, preferred_element_type=F32)
    gram = gram[:RANK] + gram[RANK : 2 * RANK] + gram[2 * RANK :]
    gram = gram[:, :RANK] + gram[:, RANK : 2 * RANK] + gram[:, 2 * RANK :]
    inverse = inverse_factor(gram)
    top = inverse.astype(BF16)
    inverse = jnp.concatenate([top, (inverse - top.astype(F32)).astype(BF16)], axis=0)
    return inverse, pieces[: 2 * RANK]


def orthonormal(diff):
    inverse, _ = factored(diff)
    return product_of(inverse, diff).astype(BF16)


def update_kernel(grown, bases, rights, out_hbm, staged, sem):
    depth, hidden = grown.shape
    edges = list(range(0, depth + 1, 256))
    copies = []
    for number, (start, stop) in enumerate(zip(edges, edges[1:])):
        rows = slice(start, stop)
        for c in range(0, hidden, 256):
            columns = slice(c, min(c + 256, hidden))
            delta = mm(bases[rows, :], rights[:, columns], NN)
            staged[rows, columns] = (grown[rows, columns].astype(F32) - delta).astype(BF16)
        span = pl.ds(start, stop - start)
        copies.append(pltpu.make_async_copy(staged.at[span], out_hbm.at[span], sem.at[number]))
        copies[-1].start()
    for copy in copies:
        copy.wait()


def make_kernel(replicas, shards, depth, hidden, tokens):
    wide = depth + tokens
    lanes = wide // shards
    blocks = [(c, min(256, hidden - c)) for c in range(0, hidden, 256)]

    def kernel(
        w_hbm, x_hbm, t_hbm, f_hbm, grown, bases_ref, rights_ref,
        f, w, x, xt, t, first, sums, gram_x,
        part0, part1, rs0, rs1, own0, own1, p_own, p0_in, p_out, p_in, v12, c_out, c_in, q_out, q_in,
        load_sem, rs_send, rs_recv, ag_send, ag_recv, x_send, x_recv,
    ):
        r, s = lax.axis_index("replica"), lax.axis_index("shard")

        def peer(dr, ds):
            return (lax.rem(r + (dr + replicas), replicas), lax.rem(s + ds, shards))

        def load(source, target, number):
            return pltpu.make_async_copy(source, target, load_sem.at[number])

        def send(source, target, send_sem, recv_sem, where):
            return pltpu.make_async_remote_copy(
                src_ref=source, dst_ref=target, send_sem=send_sem, recv_sem=recv_sem,
                device_id=where, device_id_type=MESH,
            )

        chunks = depth // CHUNK
        load_f, load_t, load_x = load(f_hbm, f, 0), load(t_hbm, t, 1), load(x_hbm, x, 2)
        load_w = [
            load(w_hbm.at[pl.ds(c * CHUNK, CHUNK)], w.at[pl.ds(c * CHUNK, CHUNK)], 3 + c)
            for c in range(chunks)
        ]
        for copy in [load_f] + load_w + [load_t, load_x]:
            copy.start()

        barrier = pltpu.get_barrier_semaphore()
        friends = [(0, o) for o in range(1, shards)]
        friends += [(1, o) for o in range(shards)] + [(-1, o) for o in range(shards)]
        friends += [(2, 0), (-2, 0), (4, 0), (-4, 0), (6, 0), (-6, 0)]
        for dr, ds in friends:
            pl.semaphore_signal(barrier, inc=1, device_id=peer(dr, ds), device_id_type=MESH)

        c_out[...] = jnp.zeros_like(c_out)
        load_f.wait()
        shared = f[...].astype(BF16)
        images = []
        for c in range(chunks):
            load_w[c].wait()
            images.append(mm(shared, w[c * CHUNK : (c + 1) * CHUNK, :], NT))
        load_t.wait()
        goal = mm(shared, t[...], NT)
        load_x.wait()
        image = jnp.concatenate(images, axis=1)
        image = image - 0.3 * mm(mm(image, x[...], NT) - goal, x[...], NN)
        image, goal = image.astype(BF16), goal.astype(BF16)
        part0[:, :depth] = image[:RANK]
        part0[:, depth:] = goal[:RANK]
        part1[:, :depth] = image[RANK:]
        part1[:, depth:] = goal[RANK:]

        def piece(ref, index):
            return ref.at[:, pl.ds(pl.multiple_of(index * lanes, 128), lanes)]

        pl.semaphore_wait(barrier, len(friends))
        scatter0, scatter1 = [], []
        for o in range(1, shards):
            where = peer(0, o)
            scatter0.append(send(piece(part0, where[1]), rs0.at[o], rs_send.at[0, o], rs_recv.at[0, o], where))
            scatter0[-1].start()
        for o in range(1, shards):
            where = peer(0, o)
            scatter1.append(send(piece(part1, where[1]), rs1.at[o], rs_send.at[1, o], rs_recv.at[1, o], where))
            scatter1[-1].start()

        for c, width in blocks:
            product = mm(x[...], w[:, c : c + width], NN) - t[:, c : c + width].astype(F32)
            first[:, c : c + width] = product
            sums[0, :, c : c + width] = product.astype(BF16)

        for copy in scatter0:
            copy.wait_recv()
        total = piece(part0, s)[...].astype(F32)
        for o in range(1, shards):
            total = total + rs0[o].astype(F32)
        own0[...] = total.astype(BF16)
        piece(p_own, s)[...] = total.astype(BF16)
        gather0 = []
        for dr, o in [(0, o) for o in range(1, shards)] + [(1, o) for o in range(shards)]:
            target = piece(p_own if dr == 0 else p0_in, s)
            number = o if dr == 0 else shards + o
            gather0.append(send(own0, target, ag_send.at[number], ag_recv.at[number], peer(dr, o)))
            gather0[-1].start()
        for copy in scatter1:
            copy.wait_recv()
        total = piece(part1, s)[...].astype(F32)
        for o in range(1, shards):
            total = total + rs1[o].astype(F32)
        own1[...] = total.astype(BF16)
        piece(v12, s)[...] = total.astype(BF16)
        gather1 = []
        for o in range(1, shards):
            number = 2 * shards + o
            gather1.append(send(own1, piece(v12, s), ag_send.at[number], ag_recv.at[number], peer(0, o)))
            gather1[-1].start()

        for c in range(chunks):
            xt[c * CHUNK : (c + 1) * CHUNK, :] = x[:, c * CHUNK : (c + 1) * CHUNK].T
        for c in range(0, tokens, 256):
            gram_x[:, c : c + 256] = mm(x[...], xt[:, c : c + 256], NN).astype(BF16)

        def next_sum(step):
            for c, width in blocks:
                last = sums[step - 1, :, c : c + width]
                product = mm(gram_x[...], last, NN)
                value = first[:, c : c + width] + last.astype(F32) - 0.3 * product
                sums[step, :, c : c + width] = value.astype(BF16)

        next_sum(1)

        def grow(c):
            rows = slice(c * CHUNK, (c + 1) * CHUNK)
            product = mm(xt[rows, :], sums[2], NN)
            grown[rows, :] = (w[rows, :].astype(F32) - 0.3 * product).astype(BF16)

        def exchange(source, target, number, distance):
            copy = send(source, target, x_send.at[number], x_recv.at[number], peer(distance, 0))
            copy.start()
            return copy

        for copy in gather0:
            copy.wait_recv()
        basis0 = orthonormal(p_own[:, :depth].astype(F32) - p0_in[:, :depth].astype(F32))
        for copy in gather1:
            copy.wait_recv()
        image = v12[:, :depth]
        inner0 = mm(image, basis0, NT)
        c_out[0, :, :RANK] = inner0
        sent_c0 = exchange(c_out.at[0], c_in.at[0], 0, 1)
        inside = mm(jnp.concatenate([image, basis0], axis=0), xt[...], NN)
        inside0 = inside[2 * RANK :]
        inside = jnp.concatenate([inside[: 2 * RANK] - v12[:, depth:].astype(F32), inside0], axis=0)
        change = 0.3 * mm(inside, x[...], NN)
        image = image.astype(F32) - change[: 2 * RANK]
        moved0 = basis0.astype(F32) - change[2 * RANK :]
        next_sum(2)
        sent_c0.wait_recv()
        inner0 = inner0 - c_in[0, :, :RANK]
        image = image - 0.5 * mm(inner0, moved0, NN)
        left1 = image[:RANK]
        p_out[0] = left1.astype(BF16)
        sent_p1 = exchange(p_out.at[0], p_in.at[0], 1, 2)

        right0 = mm(basis0, w[...], NN) - 0.3 * mm(inside0, sums[0], NN)
        q_out[0] = right0.astype(BF16)
        sent_q0 = exchange(q_out.at[0], q_in.at[0], 2, 1)
        image = image[RANK:]
        inside = mm(jnp.concatenate([image, moved0], axis=0), xt[...], NN)
        inside = jnp.concatenate([inside[:RANK] - v12[RANK:, depth:].astype(F32), inside[RANK:]], axis=0)
        change = 0.3 * mm(inside, x[...], NN)
        next_image = image - change[:RANK]
        p_out[1] = next_image.astype(BF16)
        twice0 = moved0 - change[RANK:]
        grow(0)
        grow(1)

        sent_p1.wait_recv()
        sent_p2 = exchange(p_out.at[1], p_in.at[1], 3, 4)
        basis1 = orthonormal(left1 - p_in[0].astype(F32))
        inner1 = mm(image, basis1, NT)
        c_out[1, :RANK, :RANK] = inner1
        sent_c1 = [
            exchange(c_out.at[1, pl.ds(0, RANK)], c_in.at[1 + n, pl.ds(0, RANK)], 4 + n, distance)
            for n, distance in enumerate((2, 4, 6))
        ]
        inside1 = mm(basis1, xt[...], NN)
        moved1 = basis1.astype(F32) - 0.3 * mm(inside1, x[...], NN)
        p_out[2] = moved1.astype(BF16)
        sent_m1 = exchange(p_out.at[2], p_in.at[2], 7, 4)

        right1 = mm(basis1, w[...], NN) - 0.3 * mm(inside1, sums[1], NN)
        along0 = mm(basis1, moved0, NT)
        sent_q0.wait_recv()
        right0 = right0 - q_in[0].astype(F32)
        right1 = right1 - 0.5 * mm(along0, right0, NN)
        q_out[1] = right1.astype(BF16)
        sent_q1 = exchange(q_out.at[1], q_in.at[1], 8, 2)
        for c in range(2, chunks):
            grow(c)

        sent_p2.wait_recv()
        for copy in sent_c1:
            copy.wait_recv()
        inner = inner1 - c_in[1, :RANK, :RANK]
        left2 = next_image - 0.5 * mm(inner, moved1, NN)
        inner = c_in[2, :RANK, :RANK] - c_in[3, :RANK, :RANK]
        sent_m1.wait_recv()
        left2 = left2 - (p_in[1].astype(F32) - 0.5 * mm(inner, p_in[2], NN))
        inverse, pieces = factored(left2)
        raw = mm(pieces, grown[...], NN)
        raw = raw - 0.5 * mm(mm(pieces, twice0, NT), right0, NN)
        along1 = mm(pieces, moved1, NT)
        sent_q1.wait_recv()
        right1 = right1 - q_in[1].astype(F32)
        raw = raw - 0.5 * mm(along1, right1, NN)
        raw = raw[:RANK] + raw[RANK:]
        q_out[2] = raw.astype(BF16)
        sent_q2 = exchange(q_out.at[2], q_in.at[2], 9, 4)
        c_out[2, :RANK, :RANK] = inverse[:RANK].astype(F32) + inverse[RANK:].astype(F32)
        sent_i2 = exchange(c_out.at[2, pl.ds(0, RANK)], c_in.at[4, pl.ds(0, RANK)], 10, 4)
        right2 = product_of(inverse, raw)
        basis2 = product_of(inverse, left2)
        bases_ref[...] = jnp.concatenate([twice0, moved1, basis2], axis=0).astype(BF16).T
        rights_ref[:RANK, :] = (0.5 * right0).astype(BF16)
        rights_ref[RANK : 2 * RANK, :] = (0.5 * right1).astype(BF16)
        started = scatter0 + scatter1 + gather0 + gather1
        for copy in started + sent_c1 + [sent_c0, sent_p1, sent_p2, sent_m1, sent_q0, sent_q1]:
            copy.wait_send()
        sent_i2.wait_recv()
        inverse = c_in[4, :RANK, :RANK]
        top = inverse.astype(BF16)
        inverse = jnp.concatenate([top, (inverse - top.astype(F32)).astype(BF16)], axis=0)
        sent_q2.wait_recv()
        other = mm(inverse, q_in[2], NN)
        rights_ref[2 * RANK :, :] = (0.5 * (right2 - other[:RANK] - other[RANK:])).astype(BF16)
        sent_i2.wait_send()
        sent_q2.wait_send()

    vm, dma = pltpu.VMEM, pltpu.SemaphoreType.DMA
    scratch = [
        vm((3 * RANK, hidden), F32), vm((depth, hidden), BF16), vm((tokens, depth), BF16), vm((depth, tokens), BF16),
        vm((tokens, hidden), BF16),
        vm((tokens, hidden), F32), vm((3, tokens, hidden), BF16), vm((tokens, tokens), BF16),
        vm((RANK, wide), BF16), vm((2 * RANK, wide), BF16),
        vm((shards, RANK, lanes), BF16), vm((shards, 2 * RANK, lanes), BF16),
        vm((RANK, lanes), BF16), vm((2 * RANK, lanes), BF16),
        vm((RANK, wide), BF16), vm((RANK, wide), BF16), vm((3, RANK, depth), BF16), vm((3, RANK, depth), BF16),
        vm((2 * RANK, wide), BF16),
        vm((3, 2 * RANK, 128), F32), vm((5, 2 * RANK, 128), F32),
        vm((3, RANK, hidden), BF16), vm((3, RANK, hidden), BF16),
        dma((depth // CHUNK + 3,)), dma((2, shards)), dma((2, shards)),
        dma((3 * shards,)), dma((3 * shards,)), dma((11,)), dma((11,)),
    ]
    return kernel, scratch


def solution(mesh):
    replicas, shards = mesh.shape["replica"], mesh.shape["shard"]

    def per_device(weights, x, targets, factors):
        weight = weights[0]
        depth, hidden = weight.shape
        tokens = x.shape[0]
        shared = factors.transpose(0, 2, 1).reshape(3 * RANK, hidden)
        kernel, scratch = make_kernel(replicas, shards, depth, hidden, tokens)
        in_vmem = pl.BlockSpec(memory_space=pltpu.VMEM)
        grown, bases, rights = pl.pallas_call(
            kernel,
            out_shape=(
                pltpu.VMEM((depth, hidden), BF16),
                jax.ShapeDtypeStruct((depth, 3 * RANK), BF16),
                jax.ShapeDtypeStruct((3 * RANK, hidden), BF16),
            ),
            in_specs=[pl.BlockSpec(memory_space=pltpu.HBM)] * 4,
            out_specs=(in_vmem, in_vmem, in_vmem),
            scratch_shapes=scratch,
            compiler_params=pltpu.CompilerParams(
                collective_id=0, has_side_effects=True, vmem_limit_bytes=40 * 2**20
            ),
            name="rounds",
        )(*(pltpu.with_memory_space_constraint(v, pltpu.HBM) for v in (weight, x, targets, shared)))
        return pl.pallas_call(
            update_kernel,
            out_shape=jax.ShapeDtypeStruct((depth, hidden), BF16),
            in_specs=[in_vmem] * 3,
            out_specs=pl.BlockSpec(memory_space=pltpu.HBM),
            scratch_shapes=[pltpu.VMEM((depth, hidden), BF16), pltpu.SemaphoreType.DMA((depth // 256,))],
            compiler_params=pltpu.CompilerParams(vmem_limit_bytes=16 * 2**20),
            name="update",
        )(grown, bases, rights)[None]

    in_specs = (
        P("replica", None, "shard"),
        P("replica", None),
        P("replica", "shard"),
        P(None, "shard", None),
    )
    return jax.shard_map(
        per_device, mesh=mesh, in_specs=in_specs, out_specs=P("replica", None, "shard"), check_vma=False
    )
```
